32 devices in a mesh: sweep: 4 (over y, core), sector: 8 (over z, x).
Axes of the slice: x: 2, y: 2, z: 4, core: 2. Of those that a mesh axis runs over, the one named last changes fastest.
Arguments:
- range_image: bfloat16 [4, 64, 2048, 128], P('sweep', None, 'sector'), may hold values from -6 to 6
- send_pixel: int32 [4, 8, 8, 256], P('sweep', 'sector'), may hold values from 0 to 16383, as said below
- send_cell: int32 [4, 8, 8, 256], P('sweep', 'sector'), may hold values from 0 to 255
- send_tile: int32 [4, 8, 8, 2], P('sweep', 'sector'), may hold values from 0 to 31
- send_count: int32 [4, 8, 8], P('sweep', 'sector'), may hold values from 64 to 256, as said below
- w_range: bfloat16 [3, 3, 128, 128], replicated, may hold values from -0.1875 to 0.1875
- w_proj: bfloat16 [128, 64], replicated, may hold values from -0.5 to 0.5
- w_head: bfloat16 [3, 3, 64, 64], replicated, may hold values from -0.25 to 0.25
- cotangent: bfloat16 [64, 128, 512], P(None, 'sector', 'sweep'), may hold values from -0.046875 to 0.046875
Outputs:
- head_out: bfloat16 [64, 128, 512], P(None, 'sector', 'sweep')
- grad_w_range: float32 [3, 3, 128, 128], replicated
- grad_w_proj: float32 [128, 64], replicated
- grad_w_head: float32 [3, 3, 64, 64], replicated
The draws below stay inside these ranges and needn't reach their ends.
Inputs may be any that keep to these rules, and one draw needn't show every extreme that they name: `send_pixel`: A pixel number beam * 256 + col of the sending device; the slots of one device's lists name distinct pixels. Slots q < send_count are live, the rest are padding with arbitrary pixel, cell and tile numbers; in every sweep some row band receives 256 live slots from every sector. `send_cell`: cell of a tile, numbered r * 16 + c. `send_tile`: tile of the destination's row band, numbered along the grid's columns.
All inputs are finite; a program needn't handle non-finite values.
Results may differ from the reference program's by a relative error of at most 0.0057.
Values may be sent and summed in bfloat16 or wider, within the bound.
No kernel may reach another device: no remote copies, remote signals or barrier semaphores. Data moves between devices by JAX's collectives and lax.ppermute only.
A program may use at most 192 MiB of HBM per device.

```python
import jax
import jax.numpy as jnp
from jax import lax

CHANNELS = 128
HEAD_CH = 64
BEAMS = 64
AZ_DEV = 256
TILE = 16
SLOT = 128
CAP_BLK = 2
SWEEPS = 4
SECTORS = 8
AZ = 2048
PIXELS = 16384
CAPS = 256
CELLS = 256
BAND_TILES = 32
GRID_ROWS = 128
GRID_COLS = 512


def draw_send_pixel(key, part):
    subkeys = jax.random.split(key, SWEEPS * SECTORS)

    def single_list(subkey):
        shuffled = jax.random.permutation(subkey, PIXELS)
        return shuffled[:SECTORS * CAPS].reshape(SECTORS, CAPS)
    return jax.vmap(single_list)(subkeys).reshape(SWEEPS, SECTORS, SECTORS, CAPS).astype(jnp.int32)


def draw_send_count(key, part):
    first_key = jax.random.fold_in(key, 11)
    second_key = jax.random.fold_in(key, 23)
    drawn = jax.random.randint(first_key, (SWEEPS, SECTORS, SECTORS), CAPS // 4, CAPS + 1)
    busiest = jax.random.randint(second_key, (SWEEPS, 1, 1), 0, SECTORS)
    destination = jnp.arange(SECTORS, dtype=jnp.int32)[None, None, :]
    return jnp.where(destination == busiest, CAPS, drawn).astype(jnp.int32)


def place_ends(values, own_key, low, largest):
    shape = values.shape
    index_at = [jax.random.randint(jax.random.fold_in(own_key, axis), (), 0, shape[axis]) for axis in range(len(shape))]
    values = values.at[tuple(index_at)].set(low)
    longest = shape.index(max(shape))
    index_at[longest] = (index_at[longest] + 1) % shape[longest]
    return values.at[tuple(index_at)].set(largest)


def level_of(key, dims, pieces, least, high):
    def one(axis_at, shards_of):
        steps = jax.random.uniform(jax.random.fold_in(jax.random.fold_in(key, 6), axis_at), (shards_of,), jnp.float32, least / len(pieces), high / len(pieces))
        return jnp.repeat(jnp.exp(steps), dims[axis_at] // shards_of).reshape((-1,) + (1,) * (len(dims) - axis_at - 1))

    gain = one(*pieces[0])
    for cut in pieces[1:]:
        gain = gain * one(*cut)
    return gain


def scatter_about(rng, extent, spread, most, pieces=(), kind=jnp.bfloat16):
    array = jax.random.normal(rng, extent, jnp.float32) * spread
    if len(pieces) > 0:
        array = level_of(rng, extent, pieces, -0.22, 0.18) * array
    return jnp.clip(array, min=-most, max=most).astype(kind)


def setup_inputs(seed: int = 0) -> dict:
    key_of = jax.random.split(jax.random.key(seed), 10)
    return {
        "range_image": scatter_about(key_of[0], (SWEEPS, BEAMS, AZ, CHANNELS), 1.0, 6.0, ((0, 4), (2, 8))),
        "send_pixel": draw_send_pixel(jax.random.fold_in(key_of[9], 71), 0),
        "send_cell": place_ends(jax.random.randint(key_of[2], (SWEEPS, SECTORS, SECTORS, CAPS), 0, CELLS), jax.random.fold_in(key_of[2], 1), 0, CELLS - 1).astype(jnp.int32),
        "send_tile": place_ends(jax.random.randint(key_of[3], (SWEEPS, SECTORS, SECTORS, CAP_BLK), 0, BAND_TILES), jax.random.fold_in(key_of[3], 1), 0, BAND_TILES - 1).astype(jnp.int32),
        "send_count": draw_send_count(jax.random.fold_in(key_of[9], 71), 0),
        "w_range": scatter_about(key_of[5], (3, 3, CHANNELS, CHANNELS), (9 * CHANNELS) ** -0.5, 0.1875),
        "w_proj": scatter_about(key_of[6], (CHANNELS, HEAD_CH), CHANNELS ** -0.5, 0.5),
        "w_head": scatter_about(key_of[7], (3, 3, HEAD_CH, HEAD_CH), (9 * HEAD_CH) ** -0.5, 0.25),
        "cotangent": scatter_about(key_of[8], (HEAD_CH, GRID_ROWS, GRID_COLS), (1.0 / GRID_ROWS), 0.046875, ((1, 8), (2, 4))),
    }


def silu_slope(preact):
    sigmoid = jax.nn.sigmoid(preact)
    return sigmoid * (1.0 + preact * (1.0 - sigmoid))


def to_sectors(plane):
    return plane.reshape(BEAMS, SECTORS, AZ_DEV, -1).transpose(1, 0, 2, 3).reshape(SECTORS, BEAMS * AZ_DEV, -1)


def from_sectors(grouped):
    return grouped.reshape(SECTORS, BEAMS, AZ_DEV, -1).transpose(1, 0, 2, 3).reshape(BEAMS * AZ, -1)


def range_window(padded, row_off, col_off):
    band_rows = padded[row_off:row_off + BEAMS]
    return jnp.roll(band_rows, 1 - col_off, axis=1).reshape(BEAMS * AZ, CHANNELS)


def gather_rows(table, index):
    return table[index]


def sweep_rows(sweep_image, pixels, cell_ids, tile_ids, counts, w_range):
    padded = jnp.pad(sweep_image, ((1, 1), (0, 0), (0, 0)))
    preact = jnp.zeros((BEAMS * AZ, CHANNELS), jnp.float32)
    for row_off in range(3):
        for col_off in range(3):
            preact = preact + jnp.dot(range_window(padded, row_off, col_off), w_range[row_off, col_off], preferred_element_type=jnp.float32)
    hidden = (sweep_image.reshape(BEAMS * AZ, CHANNELS).astype(jnp.float32) + jax.nn.silu(preact)).astype(jnp.bfloat16)
    grouped = to_sectors(hidden)
    live_slot = jnp.arange(CAPS, dtype=jnp.int32)[None, None, :] < counts[:, :, None]
    gathered = jax.vmap(gather_rows)(grouped, pixels)
    slot_rows = jnp.where(live_slot[..., None], gathered, jnp.zeros((), jnp.bfloat16))
    destination = jnp.arange(SECTORS, dtype=jnp.int32)[None, :, None]
    slot_tiles = jnp.repeat(tile_ids, SLOT, axis=2)
    cell_index = (destination * BAND_TILES + slot_tiles) * CELLS + cell_ids
    cell_index = jnp.where(live_slot, cell_index, SECTORS * BAND_TILES * CELLS).astype(jnp.int32)
    return padded, preact, slot_rows, live_slot, cell_index


def reference(range_image, send_pixel, send_cell, send_tile, send_count, w_range, w_proj, w_head, cotangent):
    all_cells = SECTORS * BAND_TILES * CELLS
    weights32 = w_proj.astype(jnp.float32)
    inputs_all = (range_image, send_pixel, send_cell, send_tile, send_count)

    def forward_sweep(running, inputs):
        sweep_image, pixels, cell_ids, tile_ids, counts = inputs
        _, _, slot_rows, _, cell_index = sweep_rows(sweep_image, pixels, cell_ids, tile_ids, counts, w_range)
        summed = jax.ops.segment_sum(slot_rows.reshape(-1, CHANNELS).astype(jnp.float32), cell_index.reshape(-1), num_segments=all_cells + 1)[:all_cells]
        return running + jnp.dot(summed, weights32, precision=lax.Precision.HIGHEST), None

    projected, _ = lax.scan(forward_sweep, jnp.zeros((all_cells, HEAD_CH), jnp.float32), inputs_all)
    ground = projected.astype(jnp.bfloat16).reshape(SECTORS, BAND_TILES, TILE, TILE, HEAD_CH).transpose(4, 0, 2, 1, 3).reshape(HEAD_CH, GRID_ROWS, GRID_COLS)

    ground_pad = jnp.pad(ground, ((0, 0), (1, 1), (1, 1)))
    grad_pad = jnp.pad(cotangent, ((0, 0), (1, 1), (1, 1)))
    flat_cot = cotangent.reshape(HEAD_CH, -1)
    head_sum = jnp.zeros((HEAD_CH, GRID_ROWS * GRID_COLS), jnp.float32)
    ground_grad = jnp.zeros((HEAD_CH, GRID_ROWS * GRID_COLS), jnp.float32)
    head_grads = []
    for row_off in range(3):
        for col_off in range(3):
            window = ground_pad[:, row_off:row_off + GRID_ROWS, col_off:col_off + GRID_COLS].reshape(HEAD_CH, -1)
            head_sum = head_sum + jnp.dot(w_head[row_off, col_off].T, window, preferred_element_type=jnp.float32)
            head_grads.append(lax.dot_general(window, flat_cot, (((1,), (1,)), ((), ())), preferred_element_type=jnp.float32))
            behind = grad_pad[:, 2 - row_off:2 - row_off + GRID_ROWS, 2 - col_off:2 - col_off + GRID_COLS].reshape(HEAD_CH, -1)
            ground_grad = ground_grad + jnp.dot(w_head[row_off, col_off], behind, preferred_element_type=jnp.float32)
    head_out = head_sum.astype(jnp.bfloat16).reshape(HEAD_CH, GRID_ROWS, GRID_COLS)
    grad_w_head = jnp.stack(head_grads).reshape(3, 3, HEAD_CH, HEAD_CH)
    cell_grads = ground_grad.astype(jnp.bfloat16).reshape(HEAD_CH, SECTORS, TILE, BAND_TILES, TILE).transpose(1, 3, 2, 4, 0).reshape(all_cells, HEAD_CH)

    def backward_sweep(carry, inputs):
        range_grad, proj_grad = carry
        sweep_image, pixels, cell_ids, tile_ids, counts = inputs
        padded, preact, slot_rows, live_slot, cell_index = sweep_rows(sweep_image, pixels, cell_ids, tile_ids, counts, w_range)
        picked = cell_grads[jnp.minimum(cell_index, all_cells - 1)]
        picked = jnp.where(live_slot[..., None], picked, jnp.zeros((), jnp.bfloat16))
        flat_rows = slot_rows.reshape(-1, CHANNELS)
        flat_picked = picked.reshape(-1, HEAD_CH)
        proj_grad = proj_grad + lax.dot_general(flat_rows, flat_picked, (((0,), (0,)), ((), ())), preferred_element_type=jnp.float32)
        slot_grads = jnp.dot(flat_picked, w_proj.T, preferred_element_type=jnp.float32)
        sector_base = jnp.arange(SECTORS, dtype=jnp.int32)[:, None, None] * PIXELS
        target = jnp.where(live_slot, sector_base + pixels, SECTORS * PIXELS).astype(jnp.int32)
        hidden_grad = jax.ops.segment_sum(slot_grads, target.reshape(-1), num_segments=SECTORS * PIXELS + 1)[:SECTORS * PIXELS]
        hidden_grad = from_sectors(hidden_grad.reshape(SECTORS, PIXELS, CHANNELS))
        preact_grad = (hidden_grad * silu_slope(preact)).astype(jnp.bfloat16)
        for row_off in range(3):
            for col_off in range(3):
                term = lax.dot_general(range_window(padded, row_off, col_off), preact_grad, (((0,), (0,)), ((), ())), preferred_element_type=jnp.float32)
                range_grad = range_grad.at[row_off, col_off].add(term)
        return (range_grad, proj_grad), None

    start = (jnp.zeros((3, 3, CHANNELS, CHANNELS), jnp.float32), jnp.zeros((CHANNELS, HEAD_CH), jnp.float32))
    (grad_w_range, grad_w_proj), _ = lax.scan(backward_sweep, start, inputs_all)
    return head_out, grad_w_range, grad_w_proj, grad_w_head
```

```python
import jax
import jax.numpy as jnp
from jax import lax
from jax.experimental import pallas as pl
from jax.experimental.pallas import tpu as pltpu
from jax.sharding import PartitionSpec as P

TILE = 16
CELLS = TILE * TILE
EDGE = 8
WIDE = 8
IDX_ROWS = 8
BF16 = jnp.bfloat16
F32 = jnp.float32
NT = (((1,), (1,)), ((), ()))
TN = (((0,), (0,)), ((), ()))


def dot(a, b, dims=(((1,), (0,)), ((), ()))):
    return lax.dot_general(a, b, dims, preferred_element_type=F32)


def gather_windows(base_ref, table, picked, first, slots, lines, pitch):
    def body(step, _):
        for k in range(8):
            slot = step * 8 + k
            base = base_ref[first + slot]
            for line in range(lines):
                picked[line, slot] = table[pl.ds(base + line * pitch, WIDE), :]
        return 0

    lax.fori_loop(0, slots // 8, body, 0)


def plane(picked, line, tap):
    return picked[line, :, tap, :]


def forward_kernel(
    base_ref, count_ref, image_ref, left_ref, right_ref, w_ref, wp_ref, idx_ref,
    patch_ref, slope_ref, rows_ref, send_ref, raw, table, picked, sem,
):
    step = pl.program_id(0)
    beams, columns, channels = image_ref.shape
    pitch = columns + 2 * EDGE
    slots = rows_ref.shape[0]
    chunks = raw.shape[0] // 8

    @pl.when(step == 0)
    def _():
        copies = []
        for c in range(chunks):
            part = pl.ds(c * 8, 8)
            copy = pltpu.make_async_copy(image_ref.at[part], raw.at[part], sem.at[c])
            copy.start()
            copies.append(copy)
        blank = jnp.zeros((pitch, channels), F32)
        table[pl.ds(0, pitch), :] = blank
        table[pl.ds((beams + 1) * pitch, pitch), :] = blank

        def edges(beam, _):
            line = (beam + 1) * pitch
            table[pl.ds(line + EDGE - 1, 1), :] = left_ref[pl.ds(beam, 1), :]
            table[pl.ds(line + EDGE + columns, 1), :] = right_ref[pl.ds(beam, 1), :]
            return 0

        lax.fori_loop(0, beams, edges, 0)
        for c in range(chunks):
            copies[c].wait()

            def widen(k, _):
                beam = c * 8 + k
                start = pl.multiple_of((beam + 1) * pitch + EDGE, 8)
                table[pl.ds(start, columns), :] = raw[beam].astype(F32)
                return 0

            lax.fori_loop(0, 8, widen, 0)

    @pl.when(step > 0)
    def _():
        band = step - 1
        gather_windows(base_ref, table, picked, band * slots, slots, 3, pitch)
        parts = [plane(picked, line, tap) for line in range(3) for tap in range(3)]
        patch = jnp.concatenate([p.astype(BF16) for p in parts], axis=1)
        patch_ref[...] = patch
        preact = dot(patch, w_ref[...])
        sigmoid = jax.nn.sigmoid(preact)
        slope_ref[...] = sigmoid * (1.0 + preact * (1.0 - sigmoid))
        live = lax.broadcasted_iota(jnp.int32, preact.shape, 0) < count_ref[band]
        rows = jnp.where(live, parts[4] + preact * sigmoid, 0.0).astype(BF16)
        rows_ref[...] = rows
        sent = dot(wp_ref[...], rows, NT)
        send_ref[0] = jnp.concatenate([sent, idx_ref[0]], axis=0).astype(BF16)


def forward(base, count, image, left, right, w_flat, wp_t, idx_rows):
    beams, columns, channels = image.shape
    bands, slots = base.shape
    head_ch = wp_t.shape[0]
    pitch = columns + 2 * EDGE
    taps = w_flat.shape[0]
    late = lambda i, *_: (jnp.maximum(i - 1, 0), 0)
    late3 = lambda i, *_: (jnp.maximum(i - 1, 0), 0, 0)
    whole = lambda i, *_: (0, 0)
    total = bands * slots
    return pl.pallas_call(
        forward_kernel,
        out_shape=(
            jax.ShapeDtypeStruct((total, taps), BF16),
            jax.ShapeDtypeStruct((total, channels), F32),
            jax.ShapeDtypeStruct((total, channels), BF16),
            jax.ShapeDtypeStruct((bands, head_ch + IDX_ROWS, slots), BF16),
        ),
        grid_spec=pltpu.PrefetchScalarGridSpec(
            num_scalar_prefetch=2,
            grid=(bands + 1,),
            in_specs=[
                pl.BlockSpec(memory_space=pl.ANY),
                pl.BlockSpec(left.shape, whole),
                pl.BlockSpec(right.shape, whole),
                pl.BlockSpec(w_flat.shape, whole),
                pl.BlockSpec(wp_t.shape, whole),
                pl.BlockSpec((1, IDX_ROWS, slots), late3),
            ],
            out_specs=[
                pl.BlockSpec((slots, taps), late),
                pl.BlockSpec((slots, channels), late),
                pl.BlockSpec((slots, channels), late),
                pl.BlockSpec((1, head_ch + IDX_ROWS, slots), late3),
            ],
            scratch_shapes=[
                pltpu.VMEM((beams, columns, channels), BF16),
                pltpu.VMEM(((beams + 2) * pitch, channels), F32),
                pltpu.VMEM((3, slots, WIDE, channels), F32),
                pltpu.SemaphoreType.DMA((beams // 8,)),
            ],
        ),
        compiler_params=pltpu.CompilerParams(dimension_semantics=("arbitrary",)),
        cost_estimate=pl.CostEstimate(
            flops=2 * total * taps * channels, bytes_accessed=24 << 20, transcendentals=0
        ),
        name="forward",
    )(base.reshape(-1), count, image, left, right, w_flat, wp_t, idx_rows)


def pick_kernel(base_ref, order_ref, cot_ref, wg_ref, window_ref, grad_ref, table, picked):
    step = pl.program_id(0)
    groups, lines, head_ch, columns = cot_ref.shape
    pitch = groups * columns + 2 * EDGE
    slots = window_ref.shape[0]

    @pl.when(step == 0)
    def _():
        blank = jnp.zeros((EDGE, 2 * head_ch), F32)

        def build(line, _):
            start = pl.multiple_of(line * pitch, 8)
            table[pl.ds(start, EDGE), :] = blank
            table[pl.ds(start + EDGE + groups * columns, EDGE), :] = blank
            for group in range(groups):
                held = order_ref[group]
                pair = jnp.concatenate([cot_ref[held, line], cot_ref[held, line + 1]], axis=0)
                at = pl.multiple_of(start + EDGE + group * columns, 8)
                table[pl.ds(at, columns), :] = pair.astype(F32).T
            return 0

        lax.fori_loop(0, lines - 1, build, 0)

    @pl.when(step > 0)
    def _():
        gather_windows(base_ref, table, picked, (step - 1) * slots, slots, 2, pitch)
        parts = [plane(picked, line, tap) for line in range(2) for tap in range(3)]
        window = jnp.concatenate([p.astype(BF16) for p in parts], axis=1)
        window_ref[...] = window
        grad_ref[0] = dot(wg_ref[...], window, NT).astype(BF16)


def pick(base, order, band_cot, wg):
    groups, lines, head_ch, columns = band_cot.shape
    sectors, slots = base.shape
    pitch = groups * columns + 2 * EDGE
    late = lambda i, *_: (jnp.maximum(i - 1, 0), 0)
    late3 = lambda i, *_: (jnp.maximum(i - 1, 0), 0, 0)
    total = sectors * slots
    return pl.pallas_call(
        pick_kernel,
        out_shape=(
            jax.ShapeDtypeStruct((total, 12 * head_ch), BF16),
            jax.ShapeDtypeStruct((sectors, head_ch, slots), BF16),
        ),
        grid_spec=pltpu.PrefetchScalarGridSpec(
            num_scalar_prefetch=2,
            grid=(sectors + 1,),
            in_specs=[
                pl.BlockSpec(band_cot.shape, lambda i, *_: (0, 0, 0, 0)),
                pl.BlockSpec(wg.shape, lambda i, *_: (0, 0)),
            ],
            out_specs=[
                pl.BlockSpec((slots, 12 * head_ch), late),
                pl.BlockSpec((1, head_ch, slots), late3),
            ],
            scratch_shapes=[
                pltpu.VMEM(((lines - 1) * pitch, 2 * head_ch), F32),
                pltpu.VMEM((2, slots, WIDE, 2 * head_ch), F32),
            ],
        ),
        compiler_params=pltpu.CompilerParams(dimension_semantics=("arbitrary",)),
        cost_estimate=pl.CostEstimate(
            flops=24 * total * head_ch * head_ch, bytes_accessed=12 << 20, transcendentals=0
        ),
        name="pick",
    )(base.reshape(-1), order, band_cot, wg)


def backward_kernel(
    count_ref, back_ref, sent_ref, slope_ref, rows_ref, patch_ref, window_ref, wp_ref,
    out_ref, range_acc, proj_acc, head_acc,
):
    step = pl.program_id(0)
    head_ch, slots = back_ref.shape[1:]
    channels = rows_ref.shape[1]

    @pl.when(step == 0)
    def _():
        range_acc[...] = jnp.zeros_like(range_acc)
        proj_acc[...] = jnp.zeros_like(proj_acc)
        head_acc[...] = jnp.zeros_like(head_acc)

    grads = back_ref[0]
    live = lax.broadcasted_iota(jnp.int32, grads.shape, 1) < count_ref[step]
    grads = jnp.where(live, grads.astype(F32), 0.0).astype(BF16)
    hidden_grad = dot(grads, wp_ref[...], TN)
    preact_grad = (hidden_grad * slope_ref[...]).T.astype(BF16)
    range_acc[...] += dot(preact_grad, patch_ref[...])
    proj_acc[...] += dot(grads, rows_ref[...])
    head_acc[...] += dot(sent_ref[0, :head_ch, :], window_ref[...])

    @pl.when(step == pl.num_programs(0) - 1)
    def _():
        taps = range_acc.shape[1] // channels
        for k in range(taps):
            out_ref[pl.ds(k * channels, channels), :] = (
                range_acc[:, k * channels : (k + 1) * channels].T.astype(BF16)
            )
        at = taps * channels
        out_ref[pl.ds(at, head_ch), :] = proj_acc[...].astype(BF16)
        wide = 2 * head_ch
        block = [head_acc[:, k * wide : (k + 1) * wide] for k in range(6)]
        first = lax.broadcasted_iota(jnp.int32, (head_ch, wide), 1) < head_ch
        both = jnp.where(first, pltpu.roll(block[3], head_ch, 1), block[4])
        for k, part in enumerate((block[0], block[1], block[2], both, block[5])):
            start = at + head_ch * (k + 1)
            out_ref[pl.ds(start, head_ch), :] = part.astype(BF16)


def backward(count, back, sent, slope, rows, patch, window, wp_t):
    bands, head_ch, slots = back.shape
    channels = rows.shape[1]
    taps = patch.shape[1]
    out_rows = taps + 6 * head_ch
    each = lambda i, *_: (i, 0)
    each3 = lambda i, *_: (i, 0, 0)
    total = bands * slots
    return pl.pallas_call(
        backward_kernel,
        out_shape=jax.ShapeDtypeStruct((out_rows, channels), BF16),
        grid_spec=pltpu.PrefetchScalarGridSpec(
            num_scalar_prefetch=1,
            grid=(bands,),
            in_specs=[
                pl.BlockSpec((1, head_ch, slots), each3),
                pl.BlockSpec((1,) + sent.shape[1:], each3),
                pl.BlockSpec((slots, channels), each),
                pl.BlockSpec((slots, channels), each),
                pl.BlockSpec((slots, taps), each),
                pl.BlockSpec((slots, window.shape[1]), each),
                pl.BlockSpec(wp_t.shape, lambda i, *_: (0, 0)),
            ],
            out_specs=pl.BlockSpec((out_rows, channels), lambda i, *_: (0, 0)),
            scratch_shapes=[
                pltpu.VMEM((channels, taps), F32),
                pltpu.VMEM((head_ch, channels), F32),
                pltpu.VMEM((head_ch, window.shape[1]), F32),
            ],
        ),
        compiler_params=pltpu.CompilerParams(dimension_semantics=("arbitrary",)),
        cost_estimate=pl.CostEstimate(
            flops=2 * total * taps * channels, bytes_accessed=10 << 20, transcendentals=0
        ),
        name="backward",
    )(count, back, sent, slope, rows, patch, window, wp_t)


def place_kernel(tile_ref, rows_ref, out_ref, acc):
    step = pl.program_id(0)
    tiles, head_ch, cells = acc.shape
    per_list = tile_ref.shape[0] // pl.num_programs(0)
    slot_len = rows_ref.shape[2] // per_list

    @pl.when(step == 0)
    def _():
        acc[...] = jnp.zeros_like(acc)

    for k in range(per_list):
        tile = tile_ref[step * per_list + k]

        @pl.when(jnp.logical_and(tile >= 0, tile < tiles))
        def _():
            part = rows_ref[0, :, k * slot_len : (k + 1) * slot_len]
            target = part[head_ch : head_ch + 1].astype(F32).astype(jnp.int32)
            places = lax.broadcasted_iota(jnp.int32, (cells, slot_len), 0)
            hot = jnp.where(places == target, 1.0, 0.0).astype(BF16)
            acc[tile] += dot(part[:head_ch], hot, NT)

    @pl.when(step == pl.num_programs(0) - 1)
    def _():
        out_ref[...] = acc[...].astype(BF16)


def place(tiles, rows, count, head_ch):
    lists, depth, slots = rows.shape
    return pl.pallas_call(
        place_kernel,
        out_shape=jax.ShapeDtypeStruct((count, head_ch, CELLS), BF16),
        grid_spec=pltpu.PrefetchScalarGridSpec(
            num_scalar_prefetch=1,
            grid=(lists,),
            in_specs=[pl.BlockSpec((1, depth, slots), lambda i, *_: (i, 0, 0))],
            out_specs=pl.BlockSpec((count, head_ch, CELLS), lambda i, *_: (0, 0, 0)),
            scratch_shapes=[pltpu.VMEM((count, head_ch, CELLS), F32)],
        ),
        compiler_params=pltpu.CompilerParams(dimension_semantics=("arbitrary",)),
        cost_estimate=pl.CostEstimate(
            flops=2 * lists * slots * head_ch * CELLS, bytes_accessed=2 << 20, transcendentals=0
        ),
        name="place",
    )(tiles, rows)


def gathered(block, axis):
    count = lax.axis_size(axis)
    places = jnp.arange(count, dtype=jnp.int32)
    if count & (count - 1):
        return lax.all_gather(block, axis), places
    held = block[None]
    bit = count // 2
    while bit:
        other = lax.ppermute(held, axis, [(i, i ^ bit) for i in range(count)])
        held = jnp.stack([held, other], axis=1).reshape((-1,) + block.shape)
        bit //= 2
    return held, places ^ lax.axis_index(axis)


def summed(rows, axes):
    count = 1
    for axis in axes:
        count *= lax.axis_size(axis)
    pieces = rows.reshape(count, rows.shape[0] // count, rows.shape[1])
    parts = lax.all_to_all(pieces, axes, split_axis=0, concat_axis=0, tiled=True)
    total = parts.astype(F32).sum(axis=0).astype(BF16)
    spread = jnp.broadcast_to(total[None], pieces.shape)
    return lax.all_to_all(spread, axes, split_axis=0, concat_axis=0, tiled=True).reshape(rows.shape)


def shards(
    range_image, send_pixel, send_cell, send_tile, send_count, w_range, w_proj, w_head, cotangent
):
    image = range_image[0]
    beams, columns, channels = image.shape
    head_ch, grid_rows, grid_cols = cotangent.shape
    count = send_count[0, 0]
    pixels, cells, tiles = send_pixel[0, 0], send_cell[0, 0], send_tile[0, 0]
    bands, slots = pixels.shape
    per_list = tiles.shape[1]
    sectors = lax.axis_size("sector")
    sweeps = lax.axis_size("sweep")
    sector, sweep = lax.axis_index("sector"), lax.axis_index("sweep")
    slot_tiles = jnp.repeat(tiles, slots // per_list, axis=1)

    cot_lines = cotangent.transpose(1, 0, 2)
    ahead = jnp.concatenate([image[:, columns - 1], cot_lines[grid_rows - 1]], axis=0)
    behind = jnp.concatenate([image[:, 0], cot_lines[0]], axis=0)
    from_left = lax.ppermute(ahead, "sector", [(i, (i + 1) % sectors) for i in range(sectors)])
    from_right = lax.ppermute(behind, "sector", [((i + 1) % sectors, i) for i in range(sectors)])
    targets_in = lax.all_to_all(
        slot_tiles * CELLS + cells, "sector", split_axis=0, concat_axis=0, tiled=True
    )

    none = jnp.zeros((), BF16)
    above = jnp.where(sector == 0, none, from_left[beams:])
    below = jnp.where(sector == sectors - 1, none, from_right[beams:])
    lines = jnp.concatenate([above[None], cot_lines, below[None]], axis=0)
    band_cot, order = gathered(lines, "sweep")
    band_pitch = sweeps * grid_cols + 2 * EDGE
    cell_in = targets_in % CELLS
    pick_base = (
        (cell_in // TILE) * band_pitch
        + (targets_in // CELLS) * TILE
        + cell_in % TILE
        + EDGE
        - 1
    )
    flipped = w_head[::-1, ::-1].transpose(2, 0, 1, 3)
    pair_low = jnp.concatenate([flipped[:, 0], flipped[:, 1]], axis=-1)
    pair_high = jnp.concatenate([jnp.zeros_like(flipped[:, 2]), flipped[:, 2]], axis=-1)
    wg = jnp.stack([pair_low, pair_high], axis=1).reshape(head_ch, -1)
    window, grad_out = pick(pick_base, order, band_cot, wg)
    back = lax.all_to_all(grad_out, "sector", split_axis=0, concat_axis=0, tiled=True)

    base = (pixels // columns) * (columns + 2 * EDGE) + pixels % columns + EDGE - 1
    idx_rows = jnp.pad(
        jnp.stack([cells, slot_tiles], axis=1).astype(F32), ((0, 0), (0, IDX_ROWS - 2), (0, 0))
    )
    wp_t = w_proj.T
    patch, slope, rows, sent = forward(
        base,
        count,
        image,
        from_left[:beams].astype(F32),
        from_right[:beams].astype(F32),
        w_range.reshape(-1, channels),
        wp_t,
        idx_rows,
    )
    sent_in = lax.all_to_all(sent, "sector", split_axis=0, concat_axis=0, tiled=True)

    local = backward(count, back, sent_in, slope, rows, patch, window, wp_t)
    total = summed(local, ("sweep", "sector")).astype(F32)
    taps = w_range.shape[0] * w_range.shape[1] * channels
    grad_range = total[:taps].reshape(w_range.shape)
    grad_proj = total[taps : taps + head_ch].T
    head_total = total[taps + head_ch :].reshape(5, head_ch, 2, head_ch)
    last = jnp.stack([head_total[3, :, 0], head_total[3, :, 1], head_total[4, :, 1]])
    by_a = jnp.stack([head_total[:3, :, 0], head_total[:3, :, 1], last])
    grad_head = by_a[::-1, ::-1]

    lists, _ = gathered(sent_in, "sweep")
    lists = lists.reshape((-1,) + sent_in.shape[1:])
    owned = grid_cols // TILE
    tile_rows = lists[:, head_ch + 1, :: slots // per_list].astype(jnp.int32).reshape(-1)
    ground = place(tile_rows - (sweep * owned - 1), lists, owned + 2, head_ch)
    ground = (
        ground.reshape(owned + 2, head_ch, TILE, TILE)
        .transpose(1, 2, 0, 3)
        .reshape(head_ch, TILE, (owned + 2) * TILE)[:, :, TILE - 1 : TILE + grid_cols + 1]
    )
    ground_pad = jnp.concatenate(
        [
            lax.ppermute(ground[:, -1:], "sector", [(i, i + 1) for i in range(sectors - 1)]),
            ground,
            lax.ppermute(ground[:, :1], "sector", [(i + 1, i) for i in range(sectors - 1)]),
        ],
        axis=1,
    )
    head_sum = jnp.zeros((head_ch, grid_rows * grid_cols), F32)
    for row_off in range(3):
        for col_off in range(3):
            view = ground_pad[:, row_off : row_off + grid_rows, col_off : col_off + grid_cols]
            head_sum = head_sum + dot(
                w_head[row_off, col_off].T, view.reshape(head_ch, -1)
            )
    head_out = head_sum.astype(BF16).reshape(head_ch, grid_rows, grid_cols)
    return head_out, grad_range, grad_proj, grad_head


def solution(mesh):
    return jax.shard_map(
        shards,
        mesh=mesh,
        in_specs=(
            P("sweep", None, "sector", None),
            P("sweep", "sector", None, None),
            P("sweep", "sector", None, None),
            P("sweep", "sector", None, None),
            P("sweep", "sector", None),
            P(),
            P(),
            P(),
            P(None, "sector", "sweep"),
        ),
        out_specs=(P(None, "sector", "sweep"), P(), P(), P()),
        check_vma=False,
    )
```

```python
import functools

import jax
import jax.numpy as jnp
from jax import lax
from jax.experimental import pallas as pl
from jax.experimental.pallas import tpu as pltpu
from jax.sharding import PartitionSpec as P


TILE = 16
CELLS = TILE * TILE
EDGE = 8
WIDE = 8
IDX_ROWS = 8
BF16 = jnp.bfloat16
F32 = jnp.float32
NT = (((1,), (1,)), ((), ()))
TN = (((0,), (0,)), ((), ()))


def dot(a, b, dims=(((1,), (0,)), ((), ()))):
    return lax.dot_general(a, b, dims, preferred_element_type=F32)


def gather_windows(base_ref, table, picked, first, slots, lines, pitch):
    def body(step, _):
        for k in range(8):
            slot = step * 8 + k
            base = base_ref[first + slot]
            for line in range(lines):
                at = pl.multiple_of((line * slots + slot) * WIDE, WIDE)
                picked[pl.ds(at, WIDE), :] = table[pl.ds(base + line * pitch, WIDE), :]
        return 0

    lax.fori_loop(0, slots // 8, body, 0)


def plane(picked, slots, line, tap):
    return picked[pl.ds(line * slots * WIDE + tap, slots, stride=WIDE), :]


def edges_kernel(sectors, image_ref, cot_ref, ahead_ref, behind_ref, lines_ref, raw, cot, wide, sem):
    beams, columns, channels = image_ref.shape
    head_ch, rows, grid_cols = cot_ref.shape
    span = raw.shape[2]
    sector = lax.axis_index("sector")
    cot_copy = pltpu.make_async_copy(cot_ref, cot, sem.at[2])
    cot_copy.start()
    copies = []
    for k, first in enumerate((0, columns - span)):
        part = image_ref.at[:, pl.ds(first, span), :]
        copy = pltpu.make_async_copy(part, raw.at[k], sem.at[k])
        copy.start()
        copies.append(copy)
    cot_copy.wait()
    wide[pl.ds(0, head_ch * rows), :] = cot[...].astype(F32).reshape(head_ch * rows, grid_cols)
    for row in range(rows):
        line = wide[pl.ds(row, head_ch, stride=rows), :].astype(BF16)
        lines_ref[row] = line
        if row == 0:
            behind_ref[pl.ds(beams, head_ch), :] = jnp.where(sector > 0, line, 0)
        if row == rows - 1:
            ahead_ref[pl.ds(beams, head_ch), :] = jnp.where(sector < sectors - 1, line, 0)
    for k, (out_ref, at) in enumerate(((behind_ref, 0), (ahead_ref, span - 1))):
        copies[k].wait()
        wide[pl.ds(0, beams * span), :] = raw[k].astype(F32).reshape(beams * span, channels)
        out_ref[pl.ds(0, beams), :] = wide[pl.ds(at, beams, stride=span), :].astype(BF16)


def edges(image, cot):
    beams, _, channels = image.shape
    head_ch, rows, grid_cols = cot.shape
    edge = jax.ShapeDtypeStruct((beams + head_ch, channels), BF16)
    vmem = pl.BlockSpec(memory_space=pltpu.VMEM)
    return pl.pallas_call(
        functools.partial(edges_kernel, lax.axis_size("sector")),
        out_shape=(edge, edge, jax.ShapeDtypeStruct((rows, head_ch, grid_cols), BF16)),
        in_specs=[pl.BlockSpec(memory_space=pltpu.HBM)] * 2,
        out_specs=(vmem, vmem, vmem),
        scratch_shapes=[
            pltpu.VMEM((2, beams, TILE, channels), BF16),
            pltpu.VMEM(cot.shape, BF16),
            pltpu.VMEM((max(beams * TILE, head_ch * rows), channels), F32),
            pltpu.SemaphoreType.DMA((3,)),
        ],
        compiler_params=pltpu.CompilerParams(vmem_limit_bytes=4 << 20),
        name="edges",
    )(image, cot)


def forward_kernel(
    base_ref, count_ref, image_ref, left_ref, right_ref, w_ref, wp_ref, target_ref,
    patch_ref, slope_ref, rows_ref, send_ref, raw, table, ends, picked, sem,
):
    step = pl.program_id(0)
    beams, columns, channels = image_ref.shape
    pitch = columns + 2 * EDGE
    slots = rows_ref.shape[0]
    chunks = raw.shape[0] // 8

    @pl.when(step == 0)
    def _():
        copies = []
        for c in range(chunks):
            part = pl.ds(c * 8, 8)
            copy = pltpu.make_async_copy(image_ref.at[part], raw.at[part], sem.at[c])
            copy.start()
            copies.append(copy)
        blank = jnp.zeros((pitch, channels), F32)
        table[pl.ds(0, pitch), :] = blank
        table[pl.ds((beams + 1) * pitch, pitch), :] = blank
        ends[0] = left_ref[pl.ds(0, beams), :].astype(F32)
        ends[1] = right_ref[pl.ds(0, beams), :].astype(F32)

        def sides(beam, _):
            line = (beam + 1) * pitch
            table[pl.ds(line + EDGE - 1, 1), :] = ends[0, pl.ds(beam, 1), :]
            table[pl.ds(line + EDGE + columns, 1), :] = ends[1, pl.ds(beam, 1), :]
            return 0

        lax.fori_loop(0, beams, sides, 0, unroll=8)
        for c in range(chunks):
            copies[c].wait()

            def widen(k, _):
                beam = c * 8 + k
                start = pl.multiple_of((beam + 1) * pitch + EDGE, 8)
                table[pl.ds(start, columns), :] = raw[beam].astype(F32)
                return 0

            lax.fori_loop(0, 8, widen, 0)

    @pl.when(step > 0)
    def _():
        band = step - 1
        gather_windows(base_ref, table, picked, band * slots, slots, 3, pitch)
        parts = [plane(picked, slots, line, tap) for line in range(3) for tap in range(3)]
        patch = jnp.concatenate([p.astype(BF16) for p in parts], axis=1)
        patch_ref[...] = patch
        preact = dot(patch, w_ref[...])
        sigmoid = jax.nn.sigmoid(preact)
        slope_ref[...] = sigmoid * (1.0 + preact * (1.0 - sigmoid))
        live = lax.broadcasted_iota(jnp.int32, preact.shape, 0) < count_ref[band]
        rows = jnp.where(live, parts[4] + preact * sigmoid, 0.0).astype(BF16)
        rows_ref[...] = rows
        sent = dot(wp_ref[...], rows, NT)
        target = jnp.broadcast_to(target_ref[0], (IDX_ROWS, slots))
        row = lax.broadcasted_iota(jnp.int32, target.shape, 0)
        tile = lax.div(target, CELLS)
        whole = jnp.where(row == 0, target - tile * CELLS, jnp.where(row == 1, tile, 0))
        send_ref[0, 0] = jnp.concatenate([sent, whole.astype(F32)], axis=0).astype(BF16)


def forward(base, count, image, left, right, w_flat, wp_t, targets):
    beams, columns, channels = image.shape
    bands, slots = base.shape
    head_ch = wp_t.shape[0]
    pitch = columns + 2 * EDGE
    taps = w_flat.shape[0]
    late = lambda i, *_: (jnp.maximum(i - 1, 0), 0)
    late3 = lambda i, *_: (jnp.maximum(i - 1, 0), 0, 0)
    late4 = lambda i, *_: (jnp.maximum(i - 1, 0), 0, 0, 0)
    whole = lambda i, *_: (0, 0)
    total = bands * slots
    return pl.pallas_call(
        forward_kernel,
        out_shape=(
            jax.ShapeDtypeStruct((total, taps), BF16),
            jax.ShapeDtypeStruct((total, channels), F32),
            jax.ShapeDtypeStruct((total, channels), BF16),
            jax.ShapeDtypeStruct((bands, 2, head_ch + IDX_ROWS, slots), BF16),
        ),
        grid_spec=pltpu.PrefetchScalarGridSpec(
            num_scalar_prefetch=2,
            grid=(bands + 1,),
            in_specs=[
                pl.BlockSpec(memory_space=pltpu.HBM),
                pl.BlockSpec(left.shape, whole),
                pl.BlockSpec(right.shape, whole),
                pl.BlockSpec(w_flat.shape, whole),
                pl.BlockSpec(wp_t.shape, whole),
                pl.BlockSpec((1, 1, slots), late3),
            ],
            out_specs=[
                pl.BlockSpec((slots, taps), late),
                pl.BlockSpec((slots, channels), late),
                pl.BlockSpec((slots, channels), late),
                pl.BlockSpec((1, 1, head_ch + IDX_ROWS, slots), late4),
            ],
            scratch_shapes=[
                pltpu.VMEM((beams, columns, channels), BF16),
                pltpu.VMEM(((beams + 2) * pitch, channels), F32),
                pltpu.VMEM((2, beams, channels), F32),
                pltpu.VMEM((3 * slots * WIDE, channels), F32),
                pltpu.SemaphoreType.DMA((beams // 8,)),
            ],
        ),
        compiler_params=pltpu.CompilerParams(
            dimension_semantics=("arbitrary",), vmem_limit_bytes=24 << 20
        ),
        cost_estimate=pl.CostEstimate(
            flops=2 * total * taps * channels, bytes_accessed=24 << 20, transcendentals=0
        ),
        name="forward",
    )(base.reshape(-1), count, image, left, right, w_flat, wp_t, targets[:, None])


def pick_kernel(
    base_ref, order_ref, cot_ref, wg_ref, send_ref, window_ref, grad_ref, table, picked
):
    step = pl.program_id(0)
    groups, lines, head_ch, columns = cot_ref.shape
    pitch = groups * columns + 2 * EDGE
    slots = window_ref.shape[0]

    @pl.when(step == 0)
    def _():
        blank = jnp.zeros((EDGE, 2 * head_ch), F32)

        def build(line, _):
            start = pl.multiple_of(line * pitch, 8)
            table[pl.ds(start, EDGE), :] = blank
            table[pl.ds(start + EDGE + groups * columns, EDGE), :] = blank
            for group in range(groups):
                held = order_ref[group]
                pair = jnp.concatenate([cot_ref[held, line], cot_ref[held, line + 1]], axis=0)
                at = pl.multiple_of(start + EDGE + group * columns, 8)
                table[pl.ds(at, columns), :] = pair.astype(F32).T
            return 0

        lax.fori_loop(0, lines - 1, build, 0)

    @pl.when(step > 0)
    def _():
        gather_windows(base_ref, table, picked, (step - 1) * slots, slots, 2, pitch)
        parts = [plane(picked, slots, line, tap) for line in range(2) for tap in range(3)]
        window = jnp.concatenate([p.astype(BF16) for p in parts], axis=1)
        window_ref[...] = window
        grad = dot(wg_ref[...], window, NT)
        spare = jnp.zeros((IDX_ROWS, slots), F32)
        grad_ref[0, 0] = jnp.concatenate([grad, spare], axis=0).astype(BF16)


def pick(base, order, band_cot, wg, send):
    groups, lines, head_ch, columns = band_cot.shape
    sectors, slots = base.shape
    pitch = groups * columns + 2 * EDGE
    late = lambda i, *_: (jnp.maximum(i - 1, 0), 0)
    late4 = lambda i, *_: (jnp.maximum(i - 1, 0), 1, 0, 0)
    total = sectors * slots
    return pl.pallas_call(
        pick_kernel,
        out_shape=(
            jax.ShapeDtypeStruct((total, 12 * head_ch), BF16),
            jax.ShapeDtypeStruct(send.shape, BF16),
        ),
        grid_spec=pltpu.PrefetchScalarGridSpec(
            num_scalar_prefetch=2,
            grid=(sectors + 1,),
            in_specs=[
                pl.BlockSpec(band_cot.shape, lambda i, *_: (0, 0, 0, 0)),
                pl.BlockSpec(wg.shape, lambda i, *_: (0, 0)),
                pl.BlockSpec(memory_space=pl.ANY),
            ],
            out_specs=[
                pl.BlockSpec((slots, 12 * head_ch), late),
                pl.BlockSpec((1, 1) + send.shape[2:], late4),
            ],
            scratch_shapes=[
                pltpu.VMEM(((lines - 1) * pitch, 2 * head_ch), F32),
                pltpu.VMEM((2 * slots * WIDE, 2 * head_ch), F32),
            ],
        ),
        input_output_aliases={4: 1},
        compiler_params=pltpu.CompilerParams(
            dimension_semantics=("arbitrary",), vmem_limit_bytes=16 << 20
        ),
        cost_estimate=pl.CostEstimate(
            flops=24 * total * head_ch * head_ch, bytes_accessed=12 << 20, transcendentals=0
        ),
        name="pick",
    )(base.reshape(-1), order, band_cot, wg, send)


def backward_kernel(
    count_ref, back_ref, sent_ref, slope_ref, rows_ref, patch_ref, window_ref, wp_ref,
    out_ref, range_acc, proj_acc, head_acc,
):
    step = pl.program_id(0)
    head_ch = wp_ref.shape[0]
    channels = rows_ref.shape[1]

    @pl.when(step == 0)
    def _():
        range_acc[...] = jnp.zeros_like(range_acc)
        proj_acc[...] = jnp.zeros_like(proj_acc)
        head_acc[...] = jnp.zeros_like(head_acc)

    grads = back_ref[0, 0, :head_ch, :]
    live = lax.broadcasted_iota(jnp.int32, grads.shape, 1) < count_ref[step]
    grads = jnp.where(live, grads.astype(F32), 0.0).astype(BF16)
    hidden_grad = dot(grads, wp_ref[...], TN)
    preact_grad = (hidden_grad * slope_ref[...]).T.astype(BF16)
    range_acc[...] += dot(preact_grad, patch_ref[...])
    proj_acc[...] += dot(grads, rows_ref[...])
    head_acc[...] += dot(sent_ref[0, 0, :head_ch, :], window_ref[...])

    @pl.when(step == pl.num_programs(0) - 1)
    def _():
        taps = range_acc.shape[1] // channels
        for k in range(taps):
            out_ref[pl.ds(k * channels, channels), :] = (
                range_acc[:, k * channels : (k + 1) * channels].T.astype(BF16)
            )
        at = taps * channels
        out_ref[pl.ds(at, head_ch), :] = proj_acc[...].astype(BF16)
        wide = 2 * head_ch
        block = [head_acc[:, k * wide : (k + 1) * wide] for k in range(6)]
        first = lax.broadcasted_iota(jnp.int32, (head_ch, wide), 1) < head_ch
        both = jnp.where(first, pltpu.roll(block[3], head_ch, 1), block[4])
        for k, part in enumerate((block[0], block[1], block[2], both, block[5])):
            start = at + head_ch * (k + 1)
            out_ref[pl.ds(start, head_ch), :] = part.astype(BF16)


def backward(count, mixed, slope, rows, patch, window, wp_t):
    bands, _, depth, slots = mixed.shape
    head_ch, channels = wp_t.shape
    taps = patch.shape[1]
    out_rows = taps + 6 * head_ch
    each = lambda i, *_: (i, 0)
    total = bands * slots
    return pl.pallas_call(
        backward_kernel,
        out_shape=jax.ShapeDtypeStruct((out_rows, channels), BF16),
        grid_spec=pltpu.PrefetchScalarGridSpec(
            num_scalar_prefetch=1,
            grid=(bands,),
            in_specs=[
                pl.BlockSpec((1, 1, depth, slots), lambda i, *_: (i, 1, 0, 0)),
                pl.BlockSpec((1, 1, depth, slots), lambda i, *_: (i, 0, 0, 0)),
                pl.BlockSpec((slots, channels), each),
                pl.BlockSpec((slots, channels), each),
                pl.BlockSpec((slots, taps), each),
                pl.BlockSpec((slots, window.shape[1]), each),
                pl.BlockSpec(wp_t.shape, lambda i, *_: (0, 0)),
            ],
            out_specs=pl.BlockSpec((out_rows, channels), lambda i, *_: (0, 0)),
            scratch_shapes=[
                pltpu.VMEM((channels, taps), F32),
                pltpu.VMEM((head_ch, channels), F32),
                pltpu.VMEM((head_ch, window.shape[1]), F32),
            ],
        ),
        compiler_params=pltpu.CompilerParams(
            dimension_semantics=("arbitrary",), vmem_limit_bytes=12 << 20
        ),
        cost_estimate=pl.CostEstimate(
            flops=2 * total * taps * channels, bytes_accessed=10 << 20, transcendentals=0
        ),
        name="backward",
    )(count, mixed, mixed, slope, rows, patch, window, wp_t)


def place_kernel(tile_ref, rows_ref, out_ref, acc):
    tiles, head_ch, cells = acc.shape
    lists, _, slots = rows_ref.shape
    per_list = tile_ref.shape[0] // lists
    slot_len = slots // per_list
    acc[...] = jnp.zeros_like(acc)

    def body(step, _):
        for k in range(per_list):
            tile = tile_ref[step * per_list + k]

            @pl.when(jnp.logical_and(tile >= 0, tile < tiles))
            def _():
                part = rows_ref[step, :, k * slot_len : (k + 1) * slot_len]
                target = part[head_ch : head_ch + 1].astype(F32).astype(jnp.int32)
                places = lax.broadcasted_iota(jnp.int32, (cells, slot_len), 0)
                hot = jnp.where(places == target, 1.0, 0.0).astype(BF16)
                acc[tile] += dot(part[:head_ch], hot, NT)

        return 0

    lax.fori_loop(0, lists, body, 0)
    out_ref[...] = acc[...].astype(BF16)


def place(tiles, rows, count, head_ch):
    lists, _, slots = rows.shape
    return pl.pallas_call(
        place_kernel,
        out_shape=jax.ShapeDtypeStruct((count, head_ch, CELLS), BF16),
        in_specs=[
            pl.BlockSpec(memory_space=pltpu.SMEM),
            pl.BlockSpec(memory_space=pltpu.VMEM),
        ],
        out_specs=pl.BlockSpec(memory_space=pltpu.VMEM),
        scratch_shapes=[pltpu.VMEM((count, head_ch, CELLS), F32)],
        compiler_params=pltpu.CompilerParams(vmem_limit_bytes=12 << 20),
        cost_estimate=pl.CostEstimate(
            flops=2 * lists * slots * head_ch * CELLS, bytes_accessed=2 << 20, transcendentals=0
        ),
        name="place",
    )(tiles, rows)


def gathered(block, axis):
    count = lax.axis_size(axis)
    places = jnp.arange(count, dtype=jnp.int32)
    if count & (count - 1):
        return lax.all_gather(block, axis), places
    held = block[None]
    bit = count // 2
    while bit:
        other = lax.ppermute(held, axis, [(i, i ^ bit) for i in range(count)])
        held = jnp.stack([held, other], axis=1).reshape((-1,) + block.shape)
        bit //= 2
    return held, places ^ lax.axis_index(axis)


def exchanged(block, axis):
    count = lax.axis_size(axis)
    places = jnp.arange(count, dtype=jnp.int32)
    steps = [
        lax.ppermute(block, axis, [(i, (i + k) % count) for i in range(count)])
        for k in range(1, count)
    ]
    return jnp.stack([block] + steps), (lax.axis_index(axis) - places) % count


def summed(rows, axes):
    count = 1
    for axis in axes:
        count *= lax.axis_size(axis)
    pieces = rows.reshape(count, rows.shape[0] // count, rows.shape[1])
    parts = lax.all_to_all(pieces, axes, split_axis=0, concat_axis=0, tiled=True)
    total = parts.astype(F32).sum(axis=0).astype(BF16)
    spread = jnp.broadcast_to(total[None], pieces.shape)
    spread = lax.all_to_all(spread, axes, split_axis=0, concat_axis=0, tiled=True)
    return spread.reshape(rows.shape)


def shards(
    range_image, send_pixel, send_cell, send_tile, send_count, w_range, w_proj, w_head, cotangent
):
    image = pltpu.with_memory_space_constraint(range_image[0], pltpu.HBM)
    beams, columns, channels = image.shape
    head_ch, grid_rows, grid_cols = cotangent.shape
    count = send_count[0, 0]
    pixels, cells, tiles = send_pixel[0, 0], send_cell[0, 0], send_tile[0, 0]
    _, slots = pixels.shape
    per_list = tiles.shape[1]
    sectors = lax.axis_size("sector")
    sweeps = lax.axis_size("sweep")
    sweep = lax.axis_index("sweep")
    slot_tiles = jnp.repeat(tiles, slots // per_list, axis=1)

    ahead, behind, cot_lines = edges(image, pltpu.with_memory_space_constraint(cotangent, pltpu.HBM))
    ring = [(i, (i + 1) % sectors) for i in range(sectors)]
    from_left = lax.ppermute(ahead, "sector", ring)
    from_right = lax.ppermute(behind, "sector", [(j, i) for i, j in ring])
    targets = slot_tiles * CELLS + cells
    targets_in = lax.all_to_all(targets, "sector", split_axis=0, concat_axis=0, tiled=True)

    base = (pixels // columns) * (columns + 2 * EDGE) + pixels % columns + EDGE - 1
    wp_t = w_proj.T
    lines = jnp.concatenate(
        [from_left[beams:][None], cot_lines, from_right[beams:][None]], axis=0
    )
    band_cot, order = exchanged(lines, "sweep")
    patch, slope, rows, send = forward(
        base, count, image, from_left, from_right, w_range.reshape(-1, channels), wp_t, targets
    )

    band_pitch = sweeps * grid_cols + 2 * EDGE
    cell_in = targets_in % CELLS
    pick_base = (
        (cell_in // TILE) * band_pitch
        + (targets_in // CELLS) * TILE
        + cell_in % TILE
        + EDGE
        - 1
    )
    flipped = w_head[::-1, ::-1].transpose(2, 0, 1, 3)
    pair_low = jnp.concatenate([flipped[:, 0], flipped[:, 1]], axis=-1)
    pair_high = jnp.concatenate([jnp.zeros_like(flipped[:, 2]), flipped[:, 2]], axis=-1)
    wg = jnp.stack([pair_low, pair_high], axis=1).reshape(head_ch, -1)
    window, send = pick(pick_base, order, band_cot, wg, send)
    mixed = lax.all_to_all(send, "sector", split_axis=0, concat_axis=0, tiled=True)
    sent_in = mixed[:, 0]

    lists, _ = gathered(sent_in, "sweep")
    lists = lists.reshape((-1,) + sent_in.shape[1:])
    owned = grid_cols // TILE
    tile_rows = lists[:, head_ch + 1, :: slots // per_list].astype(jnp.int32).reshape(-1)
    ground = place(tile_rows - (sweep * owned - 1), lists, owned + 2, head_ch)
    local = backward(count, mixed, slope, rows, patch, window, wp_t)
    total = summed(local, ("sweep", "sector")).astype(F32)
    taps = w_range.shape[0] * w_range.shape[1] * channels
    grad_range = total[:taps].reshape(w_range.shape)
    grad_proj = total[taps : taps + head_ch].T
    head_total = total[taps + head_ch :].reshape(5, head_ch, 2, head_ch)
    last = jnp.stack([head_total[3, :, 0], head_total[3, :, 1], head_total[4, :, 1]])
    by_a = jnp.stack([head_total[:3, :, 0], head_total[:3, :, 1], last])
    grad_head = by_a[::-1, ::-1]

    ground = (
        ground.reshape(owned + 2, head_ch, TILE, TILE)
        .transpose(1, 2, 0, 3)
        .reshape(head_ch, TILE, (owned + 2) * TILE)[:, :, TILE - 1 : TILE + grid_cols + 1]
    )
    over = lax.ppermute(ground[:, -1:], "sector", ring[:-1])
    under = lax.ppermute(ground[:, :1], "sector", [(j, i) for i, j in ring[:-1]])
    ground_pad = jnp.concatenate([over, ground, under], axis=1)
    head_sum = jnp.zeros((head_ch, grid_rows * grid_cols), F32)
    for row_off in range(3):
        for col_off in range(3):
            view = ground_pad[:, row_off : row_off + grid_rows, col_off : col_off + grid_cols]
            head_sum = head_sum + dot(
                w_head[row_off, col_off].T, view.reshape(head_ch, -1)
            )
    head_out = head_sum.astype(BF16).reshape(head_ch, grid_rows, grid_cols)
    return head_out, grad_range, grad_proj, grad_head


def solution(mesh):
    return jax.shard_map(
        shards,
        mesh=mesh,
        in_specs=(
            P("sweep", None, "sector", None),
            P("sweep", "sector", None, None),
            P("sweep", "sector", None, None),
            P("sweep", "sector", None, None),
            P("sweep", "sector", None),
            P(),
            P(),
            P(),
            P(None, "sector", "sweep"),
        ),
        out_specs=(P(None, "sector", "sweep"), P(), P(), P()),
        check_vma=False,
    )
```

```python
import functools

import jax
import jax.numpy as jnp
from jax import lax
from jax.experimental import pallas as pl
from jax.experimental.pallas import tpu as pltpu
from jax.sharding import PartitionSpec as P


TILE = 16
CELLS = TILE * TILE
EDGE = 8
WIDE = 4
IDX_ROWS = 8
BF16 = jnp.bfloat16
F32 = jnp.float32
NT = (((1,), (1,)), ((), ()))
TN = (((0,), (0,)), ((), ()))


def dot(a, b, dims=(((1,), (0,)), ((), ()))):
    return lax.dot_general(a, b, dims, preferred_element_type=F32)


def gather_slot(base_ref, table, picked, first, slot, slots, lines, pitch):
    base = base_ref[first + slot]
    for line in range(lines):
        at = (line * slots + slot) * WIDE
        if not isinstance(at, int):
            at = pl.multiple_of(at, WIDE)
        picked[pl.ds(at, WIDE), :] = table[pl.ds(base + line * pitch, WIDE), :]


def gather_windows(base_ref, table, picked, first, slots, lines, pitch):
    def body(step, _):
        for k in range(8):
            gather_slot(base_ref, table, picked, first, step * 8 + k, slots, lines, pitch)
        return 0

    lax.fori_loop(0, slots // 8, body, 0)


def in_turn(step, lists, slots, base_ref, table, buffers, lines, pitch, compute):
    now = step - 1
    first = jnp.minimum(step, lists - 1) * slots
    for parity in range(2):

        @pl.when(jnp.logical_and(step > 0, lax.rem(now, 2) == parity))
        def _():
            for slot in range(slots):
                gather_slot(
                    base_ref, table, buffers[1 - parity], first, slot, slots, lines, pitch
                )
            compute(now, buffers[parity])


def plane(picked, slots, line, tap):
    return picked[pl.ds(line * slots * WIDE + tap, slots, stride=WIDE), :]


def edges_kernel(sectors, image_ref, cot_ref, ahead_ref, behind_ref, lines_ref, raw, cot, wide, sem):
    beams, columns, channels = image_ref.shape
    head_ch, rows, grid_cols = cot_ref.shape
    span = raw.shape[2]
    sector = lax.axis_index("sector")
    cot_copy = pltpu.make_async_copy(cot_ref, cot, sem.at[2])
    cot_copy.start()
    copies = []
    for k, first in enumerate((0, columns - span)):
        part = image_ref.at[:, pl.ds(first, span), :]
        copy = pltpu.make_async_copy(part, raw.at[k], sem.at[k])
        copy.start()
        copies.append(copy)
    cot_copy.wait()
    wide[pl.ds(0, head_ch * rows), :] = cot[...].astype(F32).reshape(head_ch * rows, grid_cols)
    for row in range(rows):
        line = wide[pl.ds(row, head_ch, stride=rows), :].astype(BF16)
        lines_ref[row] = line
        if row == 0:
            behind_ref[pl.ds(beams, head_ch), :] = jnp.where(sector > 0, line, 0)
        if row == rows - 1:
            ahead_ref[pl.ds(beams, head_ch), :] = jnp.where(sector < sectors - 1, line, 0)
    for k, (out_ref, at) in enumerate(((behind_ref, 0), (ahead_ref, span - 1))):
        copies[k].wait()
        wide[pl.ds(0, beams * span), :] = raw[k].astype(F32).reshape(beams * span, channels)
        out_ref[pl.ds(0, beams), :] = wide[pl.ds(at, beams, stride=span), :].astype(BF16)


def edges(image, cot):
    beams, _, channels = image.shape
    head_ch, rows, grid_cols = cot.shape
    edge = jax.ShapeDtypeStruct((beams + head_ch, channels), BF16)
    vmem = pl.BlockSpec(memory_space=pltpu.VMEM)
    return pl.pallas_call(
        functools.partial(edges_kernel, lax.axis_size("sector")),
        out_shape=(edge, edge, jax.ShapeDtypeStruct((rows, head_ch, grid_cols), BF16)),
        in_specs=[pl.BlockSpec(memory_space=pltpu.HBM)] * 2,
        out_specs=(vmem, vmem, vmem),
        scratch_shapes=[
            pltpu.VMEM((2, beams, TILE, channels), BF16),
            pltpu.VMEM(cot.shape, BF16),
            pltpu.VMEM((max(beams * TILE, head_ch * rows), channels), F32),
            pltpu.SemaphoreType.DMA((3,)),
        ],
        compiler_params=pltpu.CompilerParams(vmem_limit_bytes=4 << 20),
        name="edges",
    )(image, cot)


def forward_kernel(
    base_ref, count_ref, image_ref, left_ref, right_ref, w_ref, wp_ref, target_ref,
    patch_ref, slope_ref, rows_ref, send_ref, raw, table, ends, even, odd, sem,
):
    step = pl.program_id(0)
    beams, columns, channels = image_ref.shape
    pitch = columns + 2 * EDGE
    slots = rows_ref.shape[0]
    chunks = raw.shape[0] // 8

    @pl.when(step == 0)
    def _():
        copies = []
        for c in range(chunks):
            part = pl.ds(c * 8, 8)
            copy = pltpu.make_async_copy(image_ref.at[part], raw.at[part], sem.at[c])
            copy.start()
            copies.append(copy)
        blank = jnp.zeros((pitch, channels), F32)
        table[pl.ds(0, pitch), :] = blank
        table[pl.ds((beams + 1) * pitch, pitch), :] = blank
        ends[0] = left_ref[pl.ds(0, beams), :].astype(F32)
        ends[1] = right_ref[pl.ds(0, beams), :].astype(F32)

        def sides(beam, _):
            line = (beam + 1) * pitch
            table[pl.ds(line + EDGE - 1, 1), :] = ends[0, pl.ds(beam, 1), :]
            table[pl.ds(line + EDGE + columns, 1), :] = ends[1, pl.ds(beam, 1), :]
            return 0

        lax.fori_loop(0, beams, sides, 0, unroll=8)
        for c in range(chunks):
            copies[c].wait()

            def widen(k, _):
                beam = c * 8 + k
                start = pl.multiple_of((beam + 1) * pitch + EDGE, 8)
                table[pl.ds(start, columns), :] = raw[beam].astype(F32)
                return 0

            lax.fori_loop(0, 8, widen, 0)
        gather_windows(base_ref, table, even, 0, slots, 3, pitch)

    def compute(band, picked):
        preact = None
        for k in range(0, 9, 2):
            parts = [plane(picked, slots, j // 3, j % 3) for j in range(k, min(k + 2, 9))]
            part = jnp.concatenate([p.astype(BF16) for p in parts], axis=1)
            columns = slice(k * channels, k * channels + part.shape[1])
            patch_ref[:, columns] = part
            term = dot(part, w_ref[columns, :])
            preact = term if preact is None else preact + term
        sigmoid = jax.nn.sigmoid(preact)
        slope_ref[...] = sigmoid * (1.0 + preact * (1.0 - sigmoid))
        live = lax.broadcasted_iota(jnp.int32, preact.shape, 0) < count_ref[band]
        rows = jnp.where(live, plane(picked, slots, 1, 1) + preact * sigmoid, 0.0).astype(BF16)
        rows_ref[...] = rows
        sent = dot(wp_ref[...], rows, NT)
        target = jnp.broadcast_to(target_ref[0], (IDX_ROWS, slots))
        row = lax.broadcasted_iota(jnp.int32, target.shape, 0)
        tile = lax.div(target, CELLS)
        whole = jnp.where(row == 0, target - tile * CELLS, jnp.where(row == 1, tile, 0))
        send_ref[0, 0] = jnp.concatenate([sent, whole.astype(F32)], axis=0).astype(BF16)

    lists = pl.num_programs(0) - 1
    in_turn(step, lists, slots, base_ref, table, (even, odd), 3, pitch, compute)


def forward(base, count, image, left, right, w_flat, wp_t, targets):
    beams, columns, channels = image.shape
    bands, slots = base.shape
    head_ch = wp_t.shape[0]
    pitch = columns + 2 * EDGE
    taps = w_flat.shape[0]
    late = lambda i, *_: (jnp.maximum(i - 1, 0), 0)
    late3 = lambda i, *_: (jnp.maximum(i - 1, 0), 0, 0)
    late4 = lambda i, *_: (jnp.maximum(i - 1, 0), 0, 0, 0)
    whole = lambda i, *_: (0, 0)
    total = bands * slots
    return pl.pallas_call(
        forward_kernel,
        out_shape=(
            jax.ShapeDtypeStruct((total, taps), BF16),
            jax.ShapeDtypeStruct((total, channels), F32),
            jax.ShapeDtypeStruct((total, channels), BF16),
            jax.ShapeDtypeStruct((bands, 2, head_ch + IDX_ROWS, slots), BF16),
        ),
        grid_spec=pltpu.PrefetchScalarGridSpec(
            num_scalar_prefetch=2,
            grid=(bands + 1,),
            in_specs=[
                pl.BlockSpec(memory_space=pltpu.HBM),
                pl.BlockSpec(left.shape, whole),
                pl.BlockSpec(right.shape, whole),
                pl.BlockSpec(w_flat.shape, whole),
                pl.BlockSpec(wp_t.shape, whole),
                pl.BlockSpec((1, 1, slots), late3),
            ],
            out_specs=[
                pl.BlockSpec((slots, taps), late),
                pl.BlockSpec((slots, channels), late),
                pl.BlockSpec((slots, channels), late),
                pl.BlockSpec((1, 1, head_ch + IDX_ROWS, slots), late4),
            ],
            scratch_shapes=[
                pltpu.VMEM((beams, columns, channels), BF16),
                pltpu.VMEM(((beams + 2) * pitch, channels), F32),
                pltpu.VMEM((2, beams, channels), F32),
                pltpu.VMEM((3 * slots * WIDE, channels), F32),
                pltpu.VMEM((3 * slots * WIDE, channels), F32),
                pltpu.SemaphoreType.DMA((beams // 8,)),
            ],
        ),
        compiler_params=pltpu.CompilerParams(
            dimension_semantics=("arbitrary",), vmem_limit_bytes=24 << 20
        ),
        cost_estimate=pl.CostEstimate(
            flops=2 * total * taps * channels, bytes_accessed=24 << 20, transcendentals=0
        ),
        name="forward",
    )(base.reshape(-1), count, image, left, right, w_flat, wp_t, targets[:, None])


def pick_kernel(
    base_ref, order_ref, cot_ref, wg_ref, send_ref, window_ref, grad_ref, table, even, odd
):
    step = pl.program_id(0)
    groups, lines, head_ch, columns = cot_ref.shape
    pitch = groups * columns + 2 * EDGE
    slots = window_ref.shape[0]

    @pl.when(step == 0)
    def _():
        blank = jnp.zeros((EDGE, 2 * head_ch), F32)

        def build(line, _):
            start = pl.multiple_of(line * pitch, 8)
            table[pl.ds(start, EDGE), :] = blank
            table[pl.ds(start + EDGE + groups * columns, EDGE), :] = blank
            for group in range(groups):
                held = order_ref[group]
                pair = jnp.concatenate([cot_ref[held, line], cot_ref[held, line + 1]], axis=0)
                at = pl.multiple_of(start + EDGE + group * columns, 8)
                table[pl.ds(at, columns), :] = pair.astype(F32).T
            return 0

        lax.fori_loop(0, lines - 1, build, 0)
        gather_windows(base_ref, table, even, 0, slots, 2, pitch)

    def compute(_, picked):
        parts = [plane(picked, slots, line, tap) for line in range(2) for tap in range(3)]
        window = jnp.concatenate([p.astype(BF16) for p in parts], axis=1)
        window_ref[...] = window
        grad = dot(wg_ref[...], window, NT)
        spare = jnp.zeros((IDX_ROWS, slots), F32)
        grad_ref[0, 0] = jnp.concatenate([grad, spare], axis=0).astype(BF16)

    lists = pl.num_programs(0) - 1
    in_turn(step, lists, slots, base_ref, table, (even, odd), 2, pitch, compute)


def pick(base, order, band_cot, wg, send):
    groups, lines, head_ch, columns = band_cot.shape
    sectors, slots = base.shape
    pitch = groups * columns + 2 * EDGE
    late = lambda i, *_: (jnp.maximum(i - 1, 0), 0)
    late4 = lambda i, *_: (jnp.maximum(i - 1, 0), 1, 0, 0)
    total = sectors * slots
    return pl.pallas_call(
        pick_kernel,
        out_shape=(
            jax.ShapeDtypeStruct((total, 12 * head_ch), BF16),
            jax.ShapeDtypeStruct(send.shape, BF16),
        ),
        grid_spec=pltpu.PrefetchScalarGridSpec(
            num_scalar_prefetch=2,
            grid=(sectors + 1,),
            in_specs=[
                pl.BlockSpec(band_cot.shape, lambda i, *_: (0, 0, 0, 0)),
                pl.BlockSpec(wg.shape, lambda i, *_: (0, 0)),
                pl.BlockSpec(memory_space=pl.ANY),
            ],
            out_specs=[
                pl.BlockSpec((slots, 12 * head_ch), late),
                pl.BlockSpec((1, 1) + send.shape[2:], late4),
            ],
            scratch_shapes=[
                pltpu.VMEM(((lines - 1) * pitch, 2 * head_ch), F32),
                pltpu.VMEM((2 * slots * WIDE, 2 * head_ch), F32),
                pltpu.VMEM((2 * slots * WIDE, 2 * head_ch), F32),
            ],
        ),
        input_output_aliases={4: 1},
        compiler_params=pltpu.CompilerParams(
            dimension_semantics=("arbitrary",), vmem_limit_bytes=14 << 20
        ),
        cost_estimate=pl.CostEstimate(
            flops=24 * total * head_ch * head_ch, bytes_accessed=12 << 20, transcendentals=0
        ),
        name="pick",
    )(base.reshape(-1), order, band_cot, wg, send)


def backward_kernel(
    count_ref, back_ref, sent_ref, slope_ref, rows_ref, patch_ref, window_ref, wp_ref,
    out_ref, range_acc, proj_acc, head_acc,
):
    step = pl.program_id(0)
    head_ch = wp_ref.shape[0]
    channels = rows_ref.shape[1]

    @pl.when(step == 0)
    def _():
        range_acc[...] = jnp.zeros_like(range_acc)
        proj_acc[...] = jnp.zeros_like(proj_acc)
        head_acc[...] = jnp.zeros_like(head_acc)

    grads = back_ref[0, 0, :head_ch, :]
    live = lax.broadcasted_iota(jnp.int32, grads.shape, 1) < count_ref[step]
    grads = jnp.where(live, grads.astype(F32), 0.0).astype(BF16)
    hidden_grad = dot(grads, wp_ref[...], TN)
    preact_grad = (hidden_grad * slope_ref[...]).T.astype(BF16)
    range_acc[...] += dot(preact_grad, patch_ref[...])
    proj_acc[...] += dot(grads, rows_ref[...])
    head_acc[...] += dot(sent_ref[0, 0, :head_ch, :], window_ref[...])

    @pl.when(step == pl.num_programs(0) - 1)
    def _():
        taps = range_acc.shape[1] // channels
        for k in range(taps):
            out_ref[pl.ds(k * channels, channels), :] = (
                range_acc[:, k * channels : (k + 1) * channels].T.astype(BF16)
            )
        at = taps * channels
        out_ref[pl.ds(at, head_ch), :] = proj_acc[...].astype(BF16)
        wide = 2 * head_ch
        block = [head_acc[:, k * wide : (k + 1) * wide] for k in range(6)]
        first = lax.broadcasted_iota(jnp.int32, (head_ch, wide), 1) < head_ch
        both = jnp.where(first, pltpu.roll(block[3], head_ch, 1), block[4])
        for k, part in enumerate((block[0], block[1], block[2], both, block[5])):
            start = at + head_ch * (k + 1)
            out_ref[pl.ds(start, head_ch), :] = part.astype(BF16)


def backward(count, mixed, slope, rows, patch, window, wp_t):
    bands, _, depth, slots = mixed.shape
    head_ch, channels = wp_t.shape
    taps = patch.shape[1]
    out_rows = taps + 6 * head_ch
    each = lambda i, *_: (i, 0)
    total = bands * slots
    return pl.pallas_call(
        backward_kernel,
        out_shape=jax.ShapeDtypeStruct((out_rows, channels), BF16),
        grid_spec=pltpu.PrefetchScalarGridSpec(
            num_scalar_prefetch=1,
            grid=(bands,),
            in_specs=[
                pl.BlockSpec((1, 1, depth, slots), lambda i, *_: (i, 1, 0, 0)),
                pl.BlockSpec((1, 1, depth, slots), lambda i, *_: (i, 0, 0, 0)),
                pl.BlockSpec((slots, channels), each),
                pl.BlockSpec((slots, channels), each),
                pl.BlockSpec((slots, taps), each),
                pl.BlockSpec((slots, window.shape[1]), each),
                pl.BlockSpec(wp_t.shape, lambda i, *_: (0, 0)),
            ],
            out_specs=pl.BlockSpec((out_rows, channels), lambda i, *_: (0, 0)),
            scratch_shapes=[
                pltpu.VMEM((channels, taps), F32),
                pltpu.VMEM((head_ch, channels), F32),
                pltpu.VMEM((head_ch, window.shape[1]), F32),
            ],
        ),
        compiler_params=pltpu.CompilerParams(
            dimension_semantics=("arbitrary",), vmem_limit_bytes=8 << 20
        ),
        cost_estimate=pl.CostEstimate(
            flops=2 * total * taps * channels, bytes_accessed=10 << 20, transcendentals=0
        ),
        name="backward",
    )(count, mixed, mixed, slope, rows, patch, window, wp_t)


def unpack_kernel(sum_ref, range_ref, proj_ref, head_ref):
    taps = range_ref.shape[0]
    head_ch = proj_ref.shape[0]
    range_ref[...] = sum_ref[pl.ds(0, taps), :].astype(F32)
    proj_ref[...] = sum_ref[pl.ds(taps, head_ch), :].astype(F32)
    for a in range(3):
        for b in range(3):
            block, half = (b, a) if a < 2 else ((3, b) if b < 2 else (4, 1))
            start = taps + head_ch * (block + 1)
            part = sum_ref[pl.ds(start, head_ch), :].astype(F32)
            head_ref[2 - a, 2 - b] = part[:, half * head_ch : (half + 1) * head_ch]


def unpack(total, taps, head_ch):
    vmem = pl.BlockSpec(memory_space=pltpu.VMEM)
    return pl.pallas_call(
        unpack_kernel,
        out_shape=(
            jax.ShapeDtypeStruct((taps, total.shape[1]), F32),
            jax.ShapeDtypeStruct((head_ch, total.shape[1]), F32),
            jax.ShapeDtypeStruct((3, 3, head_ch, head_ch), F32),
        ),
        in_specs=[vmem],
        out_specs=(vmem, vmem, vmem),
        compiler_params=pltpu.CompilerParams(vmem_limit_bytes=4 << 20),
        name="unpack",
    )(total)


def place_kernel(tile_ref, rows_ref, out_ref, acc):
    tiles, head_ch, cells = acc.shape
    lists, _, slots = rows_ref.shape
    per_list = tile_ref.shape[0] // lists
    slot_len = slots // per_list
    acc[...] = jnp.zeros_like(acc)

    def body(step, _):
        for k in range(per_list):
            tile = tile_ref[step * per_list + k]

            @pl.when(jnp.logical_and(tile >= 0, tile < tiles))
            def _():
                part = rows_ref[step, :, k * slot_len : (k + 1) * slot_len]
                target = part[head_ch : head_ch + 1].astype(F32).astype(jnp.int32)
                places = lax.broadcasted_iota(jnp.int32, (cells, slot_len), 0)
                hot = jnp.where(places == target, 1.0, 0.0).astype(BF16)
                acc[tile] += dot(part[:head_ch], hot, NT)

        return 0

    lax.fori_loop(0, lists, body, 0)
    out_ref[...] = acc[...].astype(BF16)


def place(tiles, rows, count, head_ch):
    lists, _, slots = rows.shape
    return pl.pallas_call(
        place_kernel,
        out_shape=jax.ShapeDtypeStruct((count, head_ch, CELLS), BF16),
        in_specs=[
            pl.BlockSpec(memory_space=pltpu.SMEM),
            pl.BlockSpec(memory_space=pltpu.VMEM),
        ],
        out_specs=pl.BlockSpec(memory_space=pltpu.VMEM),
        scratch_shapes=[pltpu.VMEM((count, head_ch, CELLS), F32)],
        compiler_params=pltpu.CompilerParams(vmem_limit_bytes=12 << 20),
        cost_estimate=pl.CostEstimate(
            flops=2 * lists * slots * head_ch * CELLS, bytes_accessed=2 << 20, transcendentals=0
        ),
        name="place",
    )(tiles, rows)


def gathered(block, axis):
    count = lax.axis_size(axis)
    places = jnp.arange(count, dtype=jnp.int32)
    if count & (count - 1):
        return lax.all_gather(block, axis), places
    held = block[None]
    bit = count // 2
    while bit:
        other = lax.ppermute(held, axis, [(i, i ^ bit) for i in range(count)])
        held = jnp.stack([held, other], axis=1).reshape((-1,) + block.shape)
        bit //= 2
    return held, places ^ lax.axis_index(axis)


def exchanged(block, axis):
    count = lax.axis_size(axis)
    places = jnp.arange(count, dtype=jnp.int32)
    steps = [
        lax.ppermute(block, axis, [(i, (i + k) % count) for i in range(count)])
        for k in range(1, count)
    ]
    return jnp.stack([block] + steps), (lax.axis_index(axis) - places) % count


def summed(rows, axes):
    count = 1
    for axis in axes:
        count *= lax.axis_size(axis)
    pieces = rows.reshape(count, rows.shape[0] // count, rows.shape[1])
    parts = lax.all_to_all(pieces, axes, split_axis=0, concat_axis=0, tiled=True)
    total = parts.astype(F32).sum(axis=0).astype(BF16)
    spread = jnp.broadcast_to(total[None], pieces.shape)
    spread = lax.all_to_all(spread, axes, split_axis=0, concat_axis=0, tiled=True)
    return spread.reshape(rows.shape)


def shards(
    range_image, send_pixel, send_cell, send_tile, send_count, w_range, w_proj, w_head, cotangent
):
    image = pltpu.with_memory_space_constraint(range_image[0], pltpu.HBM)
    beams, columns, channels = image.shape
    head_ch, grid_rows, grid_cols = cotangent.shape
    count = send_count[0, 0]
    pixels, cells, tiles = send_pixel[0, 0], send_cell[0, 0], send_tile[0, 0]
    _, slots = pixels.shape
    per_list = tiles.shape[1]
    sectors = lax.axis_size("sector")
    sweeps = lax.axis_size("sweep")
    sweep = lax.axis_index("sweep")
    slot_tiles = jnp.repeat(tiles, slots // per_list, axis=1)

    ahead, behind, cot_lines = edges(image, pltpu.with_memory_space_constraint(cotangent, pltpu.HBM))
    ring = [(i, (i + 1) % sectors) for i in range(sectors)]
    from_left = lax.ppermute(ahead, "sector", ring)
    from_right = lax.ppermute(behind, "sector", [(j, i) for i, j in ring])
    targets = slot_tiles * CELLS + cells
    targets_in = lax.all_to_all(targets, "sector", split_axis=0, concat_axis=0, tiled=True)

    base = (pixels // columns) * (columns + 2 * EDGE) + pixels % columns + EDGE - 1
    wp_t = w_proj.T
    lines = jnp.concatenate(
        [from_left[beams:][None], cot_lines, from_right[beams:][None]], axis=0
    )
    band_cot, order = exchanged(lines, "sweep")
    patch, slope, rows, send = forward(
        base, count, image, from_left, from_right, w_range.reshape(-1, channels), wp_t, targets
    )

    targets_in, send = lax.optimization_barrier((targets_in, send))
    band_pitch = sweeps * grid_cols + 2 * EDGE
    cell_in = targets_in % CELLS
    pick_base = (
        (cell_in // TILE) * band_pitch
        + (targets_in // CELLS) * TILE
        + cell_in % TILE
        + EDGE
        - 1
    )
    flipped = w_head[::-1, ::-1].transpose(2, 0, 1, 3)
    pair_low = jnp.concatenate([flipped[:, 0], flipped[:, 1]], axis=-1)
    pair_high = jnp.concatenate([jnp.zeros_like(flipped[:, 2]), flipped[:, 2]], axis=-1)
    wg = jnp.stack([pair_low, pair_high], axis=1).reshape(head_ch, -1)
    window, send = pick(pick_base, order, band_cot, wg, send)
    mixed = lax.all_to_all(send, "sector", split_axis=0, concat_axis=0, tiled=True)
    sent_in = mixed[:, 0]

    lists, _ = gathered(sent_in, "sweep")
    lists = lists.reshape((-1,) + sent_in.shape[1:])
    owned = grid_cols // TILE
    tile_rows = lists[:, head_ch + 1, :: slots // per_list].astype(jnp.int32).reshape(-1)
    ground = place(tile_rows - (sweep * owned - 1), lists, owned + 2, head_ch)
    local = backward(count, mixed, slope, rows, patch, window, wp_t)
    total = summed(local, ("sweep", "sector"))
    taps = w_range.shape[0] * w_range.shape[1] * channels
    grad_range, grad_proj, grad_head = unpack(total, taps, head_ch)
    grad_range = grad_range.reshape(w_range.shape)
    grad_proj = grad_proj.T

    ground = (
        ground.reshape(owned + 2, head_ch, TILE, TILE)
        .transpose(1, 2, 0, 3)
        .reshape(head_ch, TILE, (owned + 2) * TILE)[:, :, TILE - 1 : TILE + grid_cols + 1]
    )
    over = lax.ppermute(ground[:, -1:], "sector", ring[:-1])
    under = lax.ppermute(ground[:, :1], "sector", [(j, i) for i, j in ring[:-1]])
    ground_pad = jnp.concatenate([over, ground, under], axis=1)
    head_sum = jnp.zeros((head_ch, grid_rows * grid_cols), F32)
    for row_off in range(3):
        for col_off in range(3):
            view = ground_pad[:, row_off : row_off + grid_rows, col_off : col_off + grid_cols]
            head_sum = head_sum + dot(
                w_head[row_off, col_off].T, view.reshape(head_ch, -1)
            )
    head_out = head_sum.astype(BF16).reshape(head_ch, grid_rows, grid_cols)
    return head_out, grad_range, grad_proj, grad_head


def solution(mesh):
    return jax.shard_map(
        shards,
        mesh=mesh,
        in_specs=(
            P("sweep", None, "sector", None),
            P("sweep", "sector", None, None),
            P("sweep", "sector", None, None),
            P("sweep", "sector", None, None),
            P("sweep", "sector", None),
            P(),
            P(),
            P(),
            P(None, "sector", "sweep"),
        ),
        out_specs=(P(None, "sector", "sweep"), P(), P(), P()),
        check_vma=False,
    )
```

```python
import functools

import jax
import jax.numpy as jnp
from jax import lax
from jax.experimental import pallas as pl
from jax.experimental.pallas import tpu as pltpu
from jax.sharding import PartitionSpec as P


TILE = 16
CELLS = TILE * TILE
EDGE = 8
WIDE = 4
IDX_ROWS = 8
SWEEP = ("pair", "core")
GROUP = 4
BF16 = jnp.bfloat16
F32 = jnp.float32
NT = (((1,), (1,)), ((), ()))
TN = (((0,), (0,)), ((), ()))


def dot(a, b, dims=(((1,), (0,)), ((), ()))):
    return lax.dot_general(a, b, dims, preferred_element_type=F32)


def gather_slot(base_ref, table, picked, first, slot, slots, lines, pitch):
    base = base_ref[first + slot]
    for line in range(lines):
        at = (line * slots + slot) * WIDE
        if not isinstance(at, int):
            at = pl.multiple_of(at, WIDE)
        picked[pl.ds(at, WIDE), :] = table[pl.ds(base + line * pitch, WIDE), :]


def gather_windows(base_ref, table, picked, first, slots, lines, pitch):
    def body(step, _):
        for k in range(8):
            gather_slot(base_ref, table, picked, first, step * 8 + k, slots, lines, pitch)
        return 0

    lax.fori_loop(0, slots // 8, body, 0)


def in_turn(step, lists, slots, base_ref, table, buffers, lines, pitch, compute):
    now = step - 1
    first = jnp.minimum(step, lists - 1) * slots
    for parity in range(2):

        @pl.when(jnp.logical_and(step > 0, lax.rem(now, 2) == parity))
        def _():
            for slot in range(slots):
                gather_slot(
                    base_ref, table, buffers[1 - parity], first, slot, slots, lines, pitch
                )
            compute(now, buffers[parity])


def plane(picked, slots, line, tap):
    return picked[pl.ds(line * slots * WIDE + tap, slots, stride=WIDE), :]


def edges_kernel(sectors, image_ref, cot_ref, ahead_ref, behind_ref, lines_ref, raw, cot, wide, sem):
    beams, columns, channels = image_ref.shape
    head_ch, rows, grid_cols = cot_ref.shape
    span = raw.shape[2]
    sector = lax.axis_index("sector")
    cot_copy = pltpu.make_async_copy(cot_ref, cot, sem.at[2])
    cot_copy.start()
    copies = []
    for k, first in enumerate((0, columns - span)):
        part = image_ref.at[:, pl.ds(first, span), :]
        copy = pltpu.make_async_copy(part, raw.at[k], sem.at[k])
        copy.start()
        copies.append(copy)
    cot_copy.wait()
    wide[pl.ds(0, head_ch * rows), :] = cot[...].astype(F32).reshape(head_ch * rows, grid_cols)
    for row in range(rows):
        line = wide[pl.ds(row, head_ch, stride=rows), :].astype(BF16)
        lines_ref[row] = line
        if row == 0:
            behind_ref[pl.ds(beams, head_ch), :] = jnp.where(sector > 0, line, 0)
        if row == rows - 1:
            ahead_ref[pl.ds(beams, head_ch), :] = jnp.where(sector < sectors - 1, line, 0)
    for k, (out_ref, at) in enumerate(((behind_ref, 0), (ahead_ref, span - 1))):
        copies[k].wait()
        wide[pl.ds(0, beams * span), :] = raw[k].astype(F32).reshape(beams * span, channels)
        out_ref[pl.ds(0, beams), :] = wide[pl.ds(at, beams, stride=span), :].astype(BF16)


def edges(image, cot):
    beams, _, channels = image.shape
    head_ch, rows, grid_cols = cot.shape
    edge = jax.ShapeDtypeStruct((beams + head_ch, channels), BF16)
    vmem = pl.BlockSpec(memory_space=pltpu.VMEM)
    return pl.pallas_call(
        functools.partial(edges_kernel, lax.axis_size("sector")),
        out_shape=(edge, edge, jax.ShapeDtypeStruct((rows, head_ch, grid_cols), BF16)),
        in_specs=[pl.BlockSpec(memory_space=pltpu.HBM)] * 2,
        out_specs=(vmem, vmem, vmem),
        scratch_shapes=[
            pltpu.VMEM((2, beams, TILE, channels), BF16),
            pltpu.VMEM(cot.shape, BF16),
            pltpu.VMEM((max(beams * TILE, head_ch * rows), channels), F32),
            pltpu.SemaphoreType.DMA((3,)),
        ],
        compiler_params=pltpu.CompilerParams(vmem_limit_bytes=4 << 20),
        name="edges",
    )(image, cot)


def forward_kernel(
    base_ref, count_ref, image_ref, left_ref, right_ref, w_ref, wp_ref,
    patch_ref, slope_ref, rows_ref, send_ref, raw, table, ends, even, odd, sem,
):
    step = pl.program_id(0)
    beams, columns, channels = image_ref.shape
    pitch = columns + 2 * EDGE
    slots = rows_ref.shape[0]
    chunks = raw.shape[0] // 8

    @pl.when(step == 0)
    def _():
        copies = []
        for c in range(chunks):
            part = pl.ds(c * 8, 8)
            copy = pltpu.make_async_copy(image_ref.at[part], raw.at[part], sem.at[c])
            copy.start()
            copies.append(copy)
        blank = jnp.zeros((pitch, channels), F32)
        table[pl.ds(0, pitch), :] = blank
        table[pl.ds((beams + 1) * pitch, pitch), :] = blank
        ends[0] = left_ref[pl.ds(0, beams), :].astype(F32)
        ends[1] = right_ref[pl.ds(0, beams), :].astype(F32)

        def sides(beam, _):
            line = (beam + 1) * pitch
            table[pl.ds(line + EDGE - 1, 1), :] = ends[0, pl.ds(beam, 1), :]
            table[pl.ds(line + EDGE + columns, 1), :] = ends[1, pl.ds(beam, 1), :]
            return 0

        lax.fori_loop(0, beams, sides, 0, unroll=8)
        for c in range(chunks):
            copies[c].wait()

            def widen(k, _):
                beam = c * 8 + k
                start = pl.multiple_of((beam + 1) * pitch + EDGE, 8)
                table[pl.ds(start, columns), :] = raw[beam].astype(F32)
                return 0

            lax.fori_loop(0, 8, widen, 0)
        gather_windows(base_ref, table, even, 0, slots, 3, pitch)

    def compute(band, picked):
        preact = None
        for k in range(0, 9, 2):
            parts = [plane(picked, slots, j // 3, j % 3) for j in range(k, min(k + 2, 9))]
            part = jnp.concatenate([p.astype(BF16) for p in parts], axis=1)
            columns = slice(k * channels, k * channels + part.shape[1])
            patch_ref[:, columns] = part
            term = dot(part, w_ref[columns, :])
            preact = term if preact is None else preact + term
        sigmoid = jax.nn.sigmoid(preact)
        slope_ref[...] = sigmoid * (1.0 + preact * (1.0 - sigmoid))
        live = lax.broadcasted_iota(jnp.int32, preact.shape, 0) < count_ref[band]
        rows = jnp.where(live, plane(picked, slots, 1, 1) + preact * sigmoid, 0.0).astype(BF16)
        rows_ref[...] = rows
        send_ref[0, 0] = dot(wp_ref[...], rows, NT).astype(BF16)

    lists = pl.num_programs(0) - 1
    in_turn(step, lists, slots, base_ref, table, (even, odd), 3, pitch, compute)


def forward(base, count, image, left, right, w_flat, wp_t):
    beams, columns, channels = image.shape
    bands, slots = base.shape
    head_ch = wp_t.shape[0]
    pitch = columns + 2 * EDGE
    taps = w_flat.shape[0]
    late = lambda i, *_: (jnp.maximum(i - 1, 0), 0)
    late4 = lambda i, *_: (jnp.maximum(i - 1, 0), 0, 0, 0)
    whole = lambda i, *_: (0, 0)
    total = bands * slots
    return pl.pallas_call(
        forward_kernel,
        out_shape=(
            jax.ShapeDtypeStruct((total, taps), BF16),
            jax.ShapeDtypeStruct((total, channels), F32),
            jax.ShapeDtypeStruct((total, channels), BF16),
            jax.ShapeDtypeStruct((bands, 2, head_ch, slots), BF16),
        ),
        grid_spec=pltpu.PrefetchScalarGridSpec(
            num_scalar_prefetch=2,
            grid=(bands + 1,),
            in_specs=[
                pl.BlockSpec(memory_space=pltpu.HBM),
                pl.BlockSpec(left.shape, whole),
                pl.BlockSpec(right.shape, whole),
                pl.BlockSpec(w_flat.shape, whole),
                pl.BlockSpec(wp_t.shape, whole),
            ],
            out_specs=[
                pl.BlockSpec((slots, taps), late),
                pl.BlockSpec((slots, channels), late),
                pl.BlockSpec((slots, channels), late),
                pl.BlockSpec((1, 1, head_ch, slots), late4),
            ],
            scratch_shapes=[
                pltpu.VMEM((beams, columns, channels), BF16),
                pltpu.VMEM(((beams + 2) * pitch, channels), F32),
                pltpu.VMEM((2, beams, channels), F32),
                pltpu.VMEM((3 * slots * WIDE, channels), F32),
                pltpu.VMEM((3 * slots * WIDE, channels), F32),
                pltpu.SemaphoreType.DMA((beams // 8,)),
            ],
        ),
        compiler_params=pltpu.CompilerParams(
            dimension_semantics=("arbitrary",), vmem_limit_bytes=24 << 20
        ),
        cost_estimate=pl.CostEstimate(
            flops=2 * total * taps * channels, bytes_accessed=24 << 20, transcendentals=0
        ),
        name="forward",
    )(base.reshape(-1), count, image, left, right, w_flat, wp_t)


def pick_kernel(
    base_ref, order_ref, cot_ref, wg_ref, send_ref, window_ref, grad_ref, table, even, odd
):
    step = pl.program_id(0)
    groups, lines, head_ch, columns = cot_ref.shape
    pitch = groups * columns + 2 * EDGE
    slots = window_ref.shape[0]

    @pl.when(step == 0)
    def _():
        blank = jnp.zeros((EDGE, 2 * head_ch), F32)

        def build(line, _):
            start = pl.multiple_of(line * pitch, 8)
            table[pl.ds(start, EDGE), :] = blank
            table[pl.ds(start + EDGE + groups * columns, EDGE), :] = blank
            for group in range(groups):
                held = order_ref[group]
                pair = jnp.concatenate([cot_ref[held, line], cot_ref[held, line + 1]], axis=0)
                at = pl.multiple_of(start + EDGE + group * columns, 8)
                table[pl.ds(at, columns), :] = pair.astype(F32).T
            return 0

        lax.fori_loop(0, lines - 1, build, 0)
        gather_windows(base_ref, table, even, 0, slots, 2, pitch)

    def compute(_, picked):
        parts = [plane(picked, slots, line, tap) for line in range(2) for tap in range(3)]
        window = jnp.concatenate([p.astype(BF16) for p in parts], axis=1)
        window_ref[...] = window
        grad_ref[0, 0] = dot(wg_ref[...], window, NT).astype(BF16)

    lists = pl.num_programs(0) - 1
    in_turn(step, lists, slots, base_ref, table, (even, odd), 2, pitch, compute)


def pick(base, order, band_cot, wg, send):
    groups, lines, head_ch, columns = band_cot.shape
    sectors, slots = base.shape
    pitch = groups * columns + 2 * EDGE
    late = lambda i, *_: (jnp.maximum(i - 1, 0), 0)
    late4 = lambda i, *_: (jnp.maximum(i - 1, 0), 1, 0, 0)
    total = sectors * slots
    return pl.pallas_call(
        pick_kernel,
        out_shape=(
            jax.ShapeDtypeStruct((total, 12 * head_ch), BF16),
            jax.ShapeDtypeStruct(send.shape, BF16),
        ),
        grid_spec=pltpu.PrefetchScalarGridSpec(
            num_scalar_prefetch=2,
            grid=(sectors + 1,),
            in_specs=[
                pl.BlockSpec(band_cot.shape, lambda i, *_: (0, 0, 0, 0)),
                pl.BlockSpec(wg.shape, lambda i, *_: (0, 0)),
                pl.BlockSpec(memory_space=pl.ANY),
            ],
            out_specs=[
                pl.BlockSpec((slots, 12 * head_ch), late),
                pl.BlockSpec((1, 1) + send.shape[2:], late4),
            ],
            scratch_shapes=[
                pltpu.VMEM(((lines - 1) * pitch, 2 * head_ch), F32),
                pltpu.VMEM((2 * slots * WIDE, 2 * head_ch), F32),
                pltpu.VMEM((2 * slots * WIDE, 2 * head_ch), F32),
            ],
        ),
        input_output_aliases={4: 1},
        compiler_params=pltpu.CompilerParams(
            dimension_semantics=("arbitrary",), vmem_limit_bytes=14 << 20
        ),
        cost_estimate=pl.CostEstimate(
            flops=24 * total * head_ch * head_ch, bytes_accessed=12 << 20, transcendentals=0
        ),
        name="pick",
    )(base.reshape(-1), order, band_cot, wg, send)


def backward_kernel(
    count_ref, back_ref, sent_ref, slope_ref, rows_ref, patch_ref, window_ref, wp_ref,
    out_ref, range_acc, proj_acc, head_acc,
):
    step = pl.program_id(0)
    head_ch = wp_ref.shape[0]
    channels = rows_ref.shape[1]
    group = back_ref.shape[0]

    @pl.when(step == 0)
    def _():
        range_acc[...] = jnp.zeros_like(range_acc)
        proj_acc[...] = jnp.zeros_like(proj_acc)
        head_acc[...] = jnp.zeros_like(head_acc)

    lists = []
    for k in range(group):
        grads = back_ref[k, 0]
        live = lax.broadcasted_iota(jnp.int32, grads.shape, 1) < count_ref[step * group + k]
        lists.append(jnp.where(live, grads.astype(F32), 0.0).astype(BF16))
    grads = jnp.concatenate(lists, axis=1)
    sent = jnp.concatenate([sent_ref[k, 0] for k in range(group)], axis=1)
    hidden_grad = dot(grads, wp_ref[...], TN)
    preact_grad = (hidden_grad * slope_ref[...]).T.astype(BF16)
    range_acc[...] += dot(preact_grad, patch_ref[...])
    proj_acc[...] += dot(grads, rows_ref[...])
    head_acc[...] += dot(sent, window_ref[...])

    @pl.when(step == pl.num_programs(0) - 1)
    def _():
        taps = range_acc.shape[1] // channels
        for k in range(taps):
            out_ref[pl.ds(k * channels, channels), :] = (
                range_acc[:, k * channels : (k + 1) * channels].T.astype(BF16)
            )
        at = taps * channels
        out_ref[pl.ds(at, head_ch), :] = proj_acc[...].astype(BF16)
        wide = 2 * head_ch
        block = [head_acc[:, k * wide : (k + 1) * wide] for k in range(6)]
        first = lax.broadcasted_iota(jnp.int32, (head_ch, wide), 1) < head_ch
        both = jnp.where(first, pltpu.roll(block[3], head_ch, 1), block[4])
        for k, part in enumerate((block[0], block[1], block[2], both, block[5])):
            start = at + head_ch * (k + 1)
            out_ref[pl.ds(start, head_ch), :] = part.astype(BF16)


def backward(count, mixed, slope, rows, patch, window, wp_t):
    bands, _, depth, slots = mixed.shape
    head_ch, channels = wp_t.shape
    taps = patch.shape[1]
    out_rows = taps + 6 * head_ch
    each = lambda i, *_: (i, 0)
    total = bands * slots
    group = GROUP if bands % GROUP == 0 else 1
    return pl.pallas_call(
        backward_kernel,
        out_shape=jax.ShapeDtypeStruct((out_rows, channels), BF16),
        grid_spec=pltpu.PrefetchScalarGridSpec(
            num_scalar_prefetch=1,
            grid=(bands // group,),
            in_specs=[
                pl.BlockSpec((group, 1, depth, slots), lambda i, *_: (i, 1, 0, 0)),
                pl.BlockSpec((group, 1, depth, slots), lambda i, *_: (i, 0, 0, 0)),
                pl.BlockSpec((group * slots, channels), each),
                pl.BlockSpec((group * slots, channels), each),
                pl.BlockSpec((group * slots, taps), each),
                pl.BlockSpec((group * slots, window.shape[1]), each),
                pl.BlockSpec(wp_t.shape, lambda i, *_: (0, 0)),
            ],
            out_specs=pl.BlockSpec((out_rows, channels), lambda i, *_: (0, 0)),
            scratch_shapes=[
                pltpu.VMEM((channels, taps), F32),
                pltpu.VMEM((head_ch, channels), F32),
                pltpu.VMEM((head_ch, window.shape[1]), F32),
            ],
        ),
        compiler_params=pltpu.CompilerParams(
            dimension_semantics=("arbitrary",), vmem_limit_bytes=20 << 20
        ),
        cost_estimate=pl.CostEstimate(
            flops=2 * total * taps * channels, bytes_accessed=10 << 20, transcendentals=0
        ),
        name="backward",
    )(count, mixed, mixed, slope, rows, patch, window, wp_t)


def unpack_kernel(sectors, *refs):
    *held, range_ref, proj_ref, head_ref, sums = refs
    cores = len(held)
    pieces, height, _ = held[0].shape
    taps = range_ref.shape[0]
    head_ch = proj_ref.shape[0]
    me = lax.axis_index("core")
    for core in range(cores):

        @pl.when(me == core)
        def _():
            for k in range(cores):
                whose = (core - k) % cores
                for piece in range(pieces):
                    pair, sector = divmod(piece, sectors)
                    start = ((pair * cores + whose) * sectors + sector) * height
                    sums[pl.ds(start, height), :] = held[k][piece].astype(F32)

    range_ref[...] = sums[pl.ds(0, taps), :]
    proj_ref[...] = sums[pl.ds(taps, head_ch), :]
    for a in range(3):
        for b in range(3):
            block, half = (b, a) if a < 2 else ((3, b) if b < 2 else (4, 1))
            start = taps + head_ch * (block + 1)
            part = sums[pl.ds(start, head_ch), :]
            head_ref[2 - a, 2 - b] = part[:, half * head_ch : (half + 1) * head_ch]


def unpack(held, taps, head_ch):
    vmem = pl.BlockSpec(memory_space=pltpu.VMEM)
    pieces, height, channels = held[0].shape
    return pl.pallas_call(
        functools.partial(unpack_kernel, lax.axis_size("sector")),
        out_shape=(
            jax.ShapeDtypeStruct((taps, channels), F32),
            jax.ShapeDtypeStruct((head_ch, channels), F32),
            jax.ShapeDtypeStruct((3, 3, head_ch, head_ch), F32),
        ),
        in_specs=[vmem] * len(held),
        out_specs=(vmem, vmem, vmem),
        scratch_shapes=[pltpu.VMEM((len(held) * pieces * height, channels), F32)],
        compiler_params=pltpu.CompilerParams(vmem_limit_bytes=6 << 20),
        name="unpack",
    )(*held)


def place_kernel(tile_ref, rows_ref, out_ref, acc):
    tiles, head_ch, cells = acc.shape
    lists, _, slots = rows_ref.shape
    per_list = tile_ref.shape[0] // lists
    slot_len = slots // per_list
    acc[...] = jnp.zeros_like(acc)

    def body(step, _):
        for k in range(per_list):
            tile = tile_ref[step * per_list + k]

            @pl.when(jnp.logical_and(tile >= 0, tile < tiles))
            def _():
                part = rows_ref[step, :, k * slot_len : (k + 1) * slot_len]
                target = part[head_ch : head_ch + 1].astype(F32).astype(jnp.int32)
                places = lax.broadcasted_iota(jnp.int32, (cells, slot_len), 0)
                hot = jnp.where(places == target, 1.0, 0.0).astype(BF16)
                acc[tile] += dot(part[:head_ch], hot, NT)

        return 0

    lax.fori_loop(0, lists, body, 0)
    out_ref[...] = acc[...].astype(BF16)


def place(tiles, rows, count, head_ch):
    lists, _, slots = rows.shape
    return pl.pallas_call(
        place_kernel,
        out_shape=jax.ShapeDtypeStruct((count, head_ch, CELLS), BF16),
        in_specs=[
            pl.BlockSpec(memory_space=pltpu.SMEM),
            pl.BlockSpec(memory_space=pltpu.VMEM),
        ],
        out_specs=pl.BlockSpec(memory_space=pltpu.VMEM),
        scratch_shapes=[pltpu.VMEM((count, head_ch, CELLS), F32)],
        compiler_params=pltpu.CompilerParams(vmem_limit_bytes=12 << 20),
        cost_estimate=pl.CostEstimate(
            flops=2 * lists * slots * head_ch * CELLS, bytes_accessed=2 << 20, transcendentals=0
        ),
        name="place",
    )(tiles, rows)


def gathered(block, axis):
    count = lax.axis_size(axis)
    places = jnp.arange(count, dtype=jnp.int32)
    if count & (count - 1):
        return lax.all_gather(block, axis), places
    held = block[None]
    bit = count // 2
    while bit:
        other = lax.ppermute(held, axis, [(i, i ^ bit) for i in range(count)])
        held = jnp.stack([held, other], axis=1).reshape((-1,) + block.shape)
        bit //= 2
    return held, places ^ lax.axis_index(axis)


def exchanged(block, axis):
    count = lax.axis_size(axis)
    places = jnp.arange(count, dtype=jnp.int32)
    steps = []
    for k in range(1, count):
        ring = [(i, (i + k) % count) for i in range(count)]
        steps.append(lax.ppermute(block, axis, ring))
    return jnp.stack([block] + steps), (lax.axis_index(axis) - places) % count


def summed(rows):
    axes = SWEEP + ("sector",)
    count = lax.axis_size(axes)
    pieces = rows.reshape(count, rows.shape[0] // count, rows.shape[1])
    parts = lax.all_to_all(pieces, axes, split_axis=0, concat_axis=0, tiled=True)
    total = parts.astype(F32).sum(axis=0).astype(BF16)
    cores = lax.axis_size("core")
    spread = jnp.broadcast_to(total[None], (count // cores,) + total.shape)
    spread = lax.all_to_all(
        spread, ("pair", "sector"), split_axis=0, concat_axis=0, tiled=True
    )
    held = [spread]
    for k in range(1, cores):
        ring = [(i, (i + k) % cores) for i in range(cores)]
        held.append(lax.ppermute(spread, "core", ring))
    return held


def shards(
    range_image, send_pixel, send_cell, send_tile, send_count, w_range, w_proj, w_head, cotangent
):
    image = pltpu.with_memory_space_constraint(range_image[0], pltpu.HBM)
    beams, columns, channels = image.shape
    head_ch, grid_rows, grid_cols = cotangent.shape
    count = send_count[0, 0]
    pixels, cells, tiles = send_pixel[0, 0], send_cell[0, 0], send_tile[0, 0]
    _, slots = pixels.shape
    per_list = tiles.shape[1]
    sectors = lax.axis_size("sector")
    sweeps = lax.axis_size(SWEEP)
    sweep = lax.axis_index(SWEEP)
    slot_tiles = jnp.repeat(tiles, slots // per_list, axis=1)

    ahead, behind, cot_lines = edges(image, pltpu.with_memory_space_constraint(cotangent, pltpu.HBM))
    ring = [(i, (i + 1) % sectors) for i in range(sectors)]
    from_left = lax.ppermute(ahead, "sector", ring)
    from_right = lax.ppermute(behind, "sector", [(j, i) for i, j in ring])
    targets = slot_tiles * CELLS + cells
    targets_in = lax.all_to_all(targets, "sector", split_axis=0, concat_axis=0, tiled=True)

    base = (pixels // columns) * (columns + 2 * EDGE) + pixels % columns + EDGE - 1
    wp_t = w_proj.T
    lines = jnp.concatenate(
        [from_left[beams:][None], cot_lines, from_right[beams:][None]], axis=0
    )
    band_cot, order = exchanged(lines, SWEEP)
    patch, slope, rows, send = forward(
        base, count, image, from_left, from_right, w_range.reshape(-1, channels), wp_t
    )

    targets_in, send = lax.optimization_barrier((targets_in, send))
    band_pitch = sweeps * grid_cols + 2 * EDGE
    cell_in = targets_in % CELLS
    column_in = (targets_in // CELLS) * TILE + cell_in % TILE
    pick_base = (cell_in // TILE) * band_pitch + column_in + EDGE - 1
    flipped = w_head[::-1, ::-1].transpose(2, 0, 1, 3)
    pair_low = jnp.concatenate([flipped[:, 0], flipped[:, 1]], axis=-1)
    pair_high = jnp.concatenate([jnp.zeros_like(flipped[:, 2]), flipped[:, 2]], axis=-1)
    wg = jnp.stack([pair_low, pair_high], axis=1).reshape(head_ch, -1)
    window, send = pick(pick_base, order, band_cot, wg, send)
    targets_in, send = lax.optimization_barrier((targets_in, send))
    index_rows = jnp.stack([targets_in % CELLS, targets_in // CELLS], axis=1).astype(BF16)
    index_rows = jnp.pad(index_rows, ((0, 0), (0, IDX_ROWS - 2), (0, 0)))
    index_rows, send, window = lax.optimization_barrier((index_rows, send, window))
    mixed = lax.all_to_all(send, "sector", split_axis=0, concat_axis=0, tiled=True)
    sent_in = jnp.concatenate([mixed[:, 0], index_rows], axis=1)

    lists, _ = gathered(sent_in, SWEEP)
    lists = lists.reshape((-1,) + sent_in.shape[1:])
    owned = grid_cols // TILE
    tile_rows = lists[:, head_ch + 1, :: slots // per_list].astype(jnp.int32).reshape(-1)
    ground = place(tile_rows - (sweep * owned - 1), lists, owned + 2, head_ch)
    local = backward(count, mixed, slope, rows, patch, window, wp_t)
    held = summed(local)
    taps = w_range.shape[0] * w_range.shape[1] * channels
    grad_range, grad_proj, grad_head = unpack(held, taps, head_ch)
    grad_range = grad_range.reshape(w_range.shape)
    grad_proj = grad_proj.T

    ground = (
        ground.reshape(owned + 2, head_ch, TILE, TILE)
        .transpose(1, 2, 0, 3)
        .reshape(head_ch, TILE, (owned + 2) * TILE)[:, :, TILE - 1 : TILE + grid_cols + 1]
    )
    over = lax.ppermute(ground[:, -1:], "sector", ring[:-1])
    under = lax.ppermute(ground[:, :1], "sector", [(j, i) for i, j in ring[:-1]])
    ground_pad = jnp.concatenate([over, ground, under], axis=1)
    head_sum = jnp.zeros((head_ch, grid_rows * grid_cols), F32)
    for row_off in range(3):
        for col_off in range(3):
            view = ground_pad[:, row_off : row_off + grid_rows, col_off : col_off + grid_cols]
            head_sum = head_sum + dot(
                w_head[row_off, col_off].T, view.reshape(head_ch, -1)
            )
    head_out = head_sum.astype(BF16).reshape(head_ch, grid_rows, grid_cols)
    return head_out, grad_range, grad_proj, grad_head


def solution(mesh):
    sweeps, sectors = mesh.devices.shape
    cores = 2 if sweeps % 2 == 0 else 1
    devices = mesh.devices.reshape(sweeps // cores, cores, sectors)
    split = jax.sharding.Mesh(devices, SWEEP + ("sector",))
    return jax.shard_map(
        shards,
        mesh=split,
        in_specs=(
            P(SWEEP, None, "sector", None),
            P(SWEEP, "sector", None, None),
            P(SWEEP, "sector", None, None),
            P(SWEEP, "sector", None, None),
            P(SWEEP, "sector", None),
            P(),
            P(),
            P(),
            P(None, "sector", SWEEP),
        ),
        out_specs=(P(None, "sector", SWEEP), P(), P(), P()),
        check_vma=False,
    )
```

```python
import functools

import jax
import jax.numpy as jnp
from jax import lax
from jax.experimental import pallas as pl
from jax.experimental.pallas import tpu as pltpu
from jax.sharding import PartitionSpec as P


TILE = 16
CELLS = TILE * TILE
EDGE = 8
WIDE = 4
IDX_ROWS = 8
SWEEP = ("pair", "core")
GROUP = 4
BF16 = jnp.bfloat16
F32 = jnp.float32
NT = (((1,), (1,)), ((), ()))
TN = (((0,), (0,)), ((), ()))


def dot(a, b, dims=(((1,), (0,)), ((), ()))):
    return lax.dot_general(a, b, dims, preferred_element_type=F32)


def gather_slot(base_ref, table, picked, first, slot, slots, lines, pitch):
    base = base_ref[first + slot]
    for line in range(lines):
        at = (line * slots + slot) * WIDE
        if not isinstance(at, int):
            at = pl.multiple_of(at, WIDE)
        picked[pl.ds(at, WIDE), :] = table[pl.ds(base + line * pitch, WIDE), :]


def gather_windows(base_ref, table, picked, first, slots, lines, pitch):
    def body(step, _):
        for k in range(8):
            gather_slot(base_ref, table, picked, first, step * 8 + k, slots, lines, pitch)
        return 0

    lax.fori_loop(0, slots // 8, body, 0)


def in_turn(step, lists, slots, base_ref, table, buffers, lines, pitch, compute):
    now = step - 1
    first = jnp.minimum(step, lists - 1) * slots
    for parity in range(2):

        @pl.when(jnp.logical_and(step > 0, lax.rem(now, 2) == parity))
        def _():
            for slot in range(slots):
                gather_slot(
                    base_ref, table, buffers[1 - parity], first, slot, slots, lines, pitch
                )
            compute(now, buffers[parity])


def plane(picked, slots, line, tap):
    return picked[pl.ds(line * slots * WIDE + tap, slots, stride=WIDE), :]


def edges_kernel(sectors, image_ref, cot_ref, ahead_ref, behind_ref, lines_ref, raw, cot, wide, sem):
    beams, columns, channels = image_ref.shape
    head_ch, rows, grid_cols = cot_ref.shape
    span = raw.shape[2]
    sector = lax.axis_index("sector")
    cot_copy = pltpu.make_async_copy(cot_ref, cot, sem.at[2])
    cot_copy.start()
    copies = []
    for k, first in enumerate((0, columns - span)):
        part = image_ref.at[:, pl.ds(first, span), :]
        copy = pltpu.make_async_copy(part, raw.at[k], sem.at[k])
        copy.start()
        copies.append(copy)
    cot_copy.wait()
    wide[pl.ds(0, head_ch * rows), :] = cot[...].astype(F32).reshape(head_ch * rows, grid_cols)
    for row in range(rows):
        line = wide[pl.ds(row, head_ch, stride=rows), :].astype(BF16)
        lines_ref[row] = line
        if row == 0:
            behind_ref[pl.ds(beams, head_ch), :] = jnp.where(sector > 0, line, 0)
        if row == rows - 1:
            ahead_ref[pl.ds(beams, head_ch), :] = jnp.where(sector < sectors - 1, line, 0)
    for k, (out_ref, at) in enumerate(((behind_ref, 0), (ahead_ref, span - 1))):
        copies[k].wait()
        wide[pl.ds(0, beams * span), :] = raw[k].astype(F32).reshape(beams * span, channels)
        out_ref[pl.ds(0, beams), :] = wide[pl.ds(at, beams, stride=span), :].astype(BF16)


def edges(image, cot):
    beams, _, channels = image.shape
    head_ch, rows, grid_cols = cot.shape
    edge = jax.ShapeDtypeStruct((beams + head_ch, channels), BF16)
    vmem = pl.BlockSpec(memory_space=pltpu.VMEM)
    return pl.pallas_call(
        functools.partial(edges_kernel, lax.axis_size("sector")),
        out_shape=(edge, edge, jax.ShapeDtypeStruct((rows, head_ch, grid_cols), BF16)),
        in_specs=[pl.BlockSpec(memory_space=pltpu.HBM)] * 2,
        out_specs=(vmem, vmem, vmem),
        scratch_shapes=[
            pltpu.VMEM((2, beams, TILE, channels), BF16),
            pltpu.VMEM(cot.shape, BF16),
            pltpu.VMEM((max(beams * TILE, head_ch * rows) + EDGE, channels), F32),
            pltpu.SemaphoreType.DMA((3,)),
        ],
        compiler_params=pltpu.CompilerParams(vmem_limit_bytes=4 << 20),
        name="edges",
    )(image, cot)


def forward_kernel(
    base_ref, count_ref, image_ref, left_ref, right_ref, w_ref, wp_ref,
    patch_ref, slope_ref, rows_ref, send_ref, raw, table, ends, even, odd, sem,
):
    step = pl.program_id(0)
    beams, columns, channels = image_ref.shape
    pitch = columns + 2 * EDGE
    slots = rows_ref.shape[0]
    chunks = raw.shape[0] // 8

    @pl.when(step == 0)
    def _():
        copies = []
        for c in range(chunks):
            part = pl.ds(c * 8, 8)
            copy = pltpu.make_async_copy(image_ref.at[part], raw.at[part], sem.at[c])
            copy.start()
            copies.append(copy)
        blank = jnp.zeros((pitch, channels), F32)
        table[pl.ds(0, pitch), :] = blank
        table[pl.ds((beams + 1) * pitch, pitch), :] = blank
        ends[0, pl.ds(0, beams), :] = left_ref[pl.ds(0, beams), :].astype(F32)
        ends[1, pl.ds(0, beams), :] = right_ref[pl.ds(0, beams), :].astype(F32)

        def sides(beam, _):
            line = (beam + 1) * pitch
            table[pl.ds(line + EDGE - 1, 1), :] = ends[0, pl.ds(beam, 1), :]
            table[pl.ds(line + EDGE + columns, 1), :] = ends[1, pl.ds(beam, 1), :]
            return 0

        lax.fori_loop(0, beams, sides, 0, unroll=8)
        for c in range(chunks):
            copies[c].wait()

            def widen(k, _):
                beam = c * 8 + k
                start = pl.multiple_of((beam + 1) * pitch + EDGE, 8)
                table[pl.ds(start, columns), :] = raw[beam].astype(F32)
                return 0

            lax.fori_loop(0, 8, widen, 0)
        gather_windows(base_ref, table, even, 0, slots, 3, pitch)

    def compute(band, picked):
        preact = None
        for k in range(0, 9, 2):
            parts = [plane(picked, slots, j // 3, j % 3) for j in range(k, min(k + 2, 9))]
            part = jnp.concatenate([p.astype(BF16) for p in parts], axis=1)
            columns = slice(k * channels, k * channels + part.shape[1])
            patch_ref[:, columns] = part
            term = dot(part, w_ref[columns, :])
            preact = term if preact is None else preact + term
        sigmoid = jax.nn.sigmoid(preact)
        slope_ref[...] = sigmoid * (1.0 + preact * (1.0 - sigmoid))
        live = lax.broadcasted_iota(jnp.int32, preact.shape, 0) < count_ref[band]
        rows = jnp.where(live, plane(picked, slots, 1, 1) + preact * sigmoid, 0.0).astype(BF16)
        rows_ref[...] = rows
        send_ref[0, 0] = dot(wp_ref[...], rows, NT).astype(BF16)

    lists = pl.num_programs(0) - 1
    in_turn(step, lists, slots, base_ref, table, (even, odd), 3, pitch, compute)


def forward(base, count, image, left, right, w_flat, wp_t):
    beams, columns, channels = image.shape
    bands, slots = base.shape
    head_ch = wp_t.shape[0]
    pitch = columns + 2 * EDGE
    taps = w_flat.shape[0]
    late = lambda i, *_: (jnp.maximum(i - 1, 0), 0)
    late4 = lambda i, *_: (jnp.maximum(i - 1, 0), 0, 0, 0)
    whole = lambda i, *_: (0, 0)
    total = bands * slots
    return pl.pallas_call(
        forward_kernel,
        out_shape=(
            jax.ShapeDtypeStruct((total, taps), BF16),
            jax.ShapeDtypeStruct((total, channels), F32),
            jax.ShapeDtypeStruct((total, channels), BF16),
            jax.ShapeDtypeStruct((bands, 2, head_ch, slots), BF16),
        ),
        grid_spec=pltpu.PrefetchScalarGridSpec(
            num_scalar_prefetch=2,
            grid=(bands + 1,),
            in_specs=[
                pl.BlockSpec(memory_space=pltpu.HBM),
                pl.BlockSpec(left.shape, whole),
                pl.BlockSpec(right.shape, whole),
                pl.BlockSpec(w_flat.shape, whole),
                pl.BlockSpec(wp_t.shape, whole),
            ],
            out_specs=[
                pl.BlockSpec((slots, taps), late),
                pl.BlockSpec((slots, channels), late),
                pl.BlockSpec((slots, channels), late),
                pl.BlockSpec((1, 1, head_ch, slots), late4),
            ],
            scratch_shapes=[
                pltpu.VMEM((beams, columns, channels), BF16),
                pltpu.VMEM(((beams + 2) * pitch + EDGE, channels), F32),
                pltpu.VMEM((2, beams + EDGE, channels), F32),
                pltpu.VMEM((3 * slots * WIDE + EDGE, channels), F32),
                pltpu.VMEM((3 * slots * WIDE + EDGE, channels), F32),
                pltpu.SemaphoreType.DMA((beams // 8,)),
            ],
        ),
        compiler_params=pltpu.CompilerParams(
            dimension_semantics=("arbitrary",), vmem_limit_bytes=24 << 20
        ),
        cost_estimate=pl.CostEstimate(
            flops=2 * total * taps * channels, bytes_accessed=24 << 20, transcendentals=0
        ),
        name="forward",
    )(base.reshape(-1), count, image, left, right, w_flat, wp_t)


def pick_kernel(
    base_ref, order_ref, cot_ref, wg_ref, send_ref, window_ref, grad_ref, table, even, odd
):
    step = pl.program_id(0)
    groups, lines, head_ch, columns = cot_ref.shape
    pitch = groups * columns + 2 * EDGE
    slots = window_ref.shape[0]

    @pl.when(step == 0)
    def _():
        blank = jnp.zeros((EDGE, 2 * head_ch), F32)

        def build(line, _):
            start = pl.multiple_of(line * pitch, 8)
            table[pl.ds(start, EDGE), :] = blank
            table[pl.ds(start + EDGE + groups * columns, EDGE), :] = blank
            for group in range(groups):
                held = order_ref[group]
                pair = jnp.concatenate([cot_ref[held, line], cot_ref[held, line + 1]], axis=0)
                at = pl.multiple_of(start + EDGE + group * columns, 8)
                table[pl.ds(at, columns), :] = pair.astype(F32).T
            return 0

        lax.fori_loop(0, lines - 1, build, 0)
        gather_windows(base_ref, table, even, 0, slots, 2, pitch)

    def compute(_, picked):
        parts = [plane(picked, slots, line, tap) for line in range(2) for tap in range(3)]
        window = jnp.concatenate([p.astype(BF16) for p in parts], axis=1)
        window_ref[...] = window
        grad_ref[0, 0] = dot(wg_ref[...], window, NT).astype(BF16)

    lists = pl.num_programs(0) - 1
    in_turn(step, lists, slots, base_ref, table, (even, odd), 2, pitch, compute)


def pick(base, order, band_cot, wg, send):
    groups, lines, head_ch, columns = band_cot.shape
    sectors, slots = base.shape
    pitch = groups * columns + 2 * EDGE
    late = lambda i, *_: (jnp.maximum(i - 1, 0), 0)
    late4 = lambda i, *_: (jnp.maximum(i - 1, 0), 1, 0, 0)
    total = sectors * slots
    return pl.pallas_call(
        pick_kernel,
        out_shape=(
            jax.ShapeDtypeStruct((total, 12 * head_ch), BF16),
            jax.ShapeDtypeStruct(send.shape, BF16),
        ),
        grid_spec=pltpu.PrefetchScalarGridSpec(
            num_scalar_prefetch=2,
            grid=(sectors + 1,),
            in_specs=[
                pl.BlockSpec(band_cot.shape, lambda i, *_: (0, 0, 0, 0)),
                pl.BlockSpec(wg.shape, lambda i, *_: (0, 0)),
                pl.BlockSpec(memory_space=pl.ANY),
            ],
            out_specs=[
                pl.BlockSpec((slots, 12 * head_ch), late),
                pl.BlockSpec((1, 1) + send.shape[2:], late4),
            ],
            scratch_shapes=[
                pltpu.VMEM(((lines - 1) * pitch + EDGE, 2 * head_ch), F32),
                pltpu.VMEM((2 * slots * WIDE + EDGE, 2 * head_ch), F32),
                pltpu.VMEM((2 * slots * WIDE + EDGE, 2 * head_ch), F32),
            ],
        ),
        input_output_aliases={4: 1},
        compiler_params=pltpu.CompilerParams(
            dimension_semantics=("arbitrary",), vmem_limit_bytes=14 << 20
        ),
        cost_estimate=pl.CostEstimate(
            flops=24 * total * head_ch * head_ch, bytes_accessed=12 << 20, transcendentals=0
        ),
        name="pick",
    )(base.reshape(-1), order, band_cot, wg, send)


def backward_kernel(
    count_ref, back_ref, sent_ref, slope_ref, rows_ref, patch_ref, window_ref, wp_ref,
    out_ref, range_acc, proj_acc, head_acc,
):
    step = pl.program_id(0)
    head_ch = wp_ref.shape[0]
    channels = rows_ref.shape[1]
    group = back_ref.shape[0]

    @pl.when(step == 0)
    def _():
        range_acc[...] = jnp.zeros_like(range_acc)
        proj_acc[...] = jnp.zeros_like(proj_acc)
        head_acc[...] = jnp.zeros_like(head_acc)

    lists = []
    for k in range(group):
        grads = back_ref[k, 0]
        live = lax.broadcasted_iota(jnp.int32, grads.shape, 1) < count_ref[step * group + k]
        lists.append(jnp.where(live, grads.astype(F32), 0.0).astype(BF16))
    grads = jnp.concatenate(lists, axis=1)
    sent = jnp.concatenate([sent_ref[k, 0] for k in range(group)], axis=1)
    hidden_grad = dot(grads, wp_ref[...], TN)
    preact_grad = (hidden_grad * slope_ref[...]).T.astype(BF16)
    range_acc[...] += dot(preact_grad, patch_ref[...])
    proj_acc[...] += dot(grads, rows_ref[...])
    head_acc[...] += dot(sent, window_ref[...])

    @pl.when(step == pl.num_programs(0) - 1)
    def _():
        taps = range_acc.shape[1] // channels
        for k in range(taps):
            out_ref[pl.ds(k * channels, channels), :] = (
                range_acc[:, k * channels : (k + 1) * channels].T.astype(BF16)
            )
        at = taps * channels
        out_ref[pl.ds(at, head_ch), :] = proj_acc[...].astype(BF16)
        wide = 2 * head_ch
        block = [head_acc[:, k * wide : (k + 1) * wide] for k in range(6)]
        first = lax.broadcasted_iota(jnp.int32, (head_ch, wide), 1) < head_ch
        both = jnp.where(first, pltpu.roll(block[3], head_ch, 1), block[4])
        for k, part in enumerate((block[0], block[1], block[2], both, block[5])):
            start = at + head_ch * (k + 1)
            out_ref[pl.ds(start, head_ch), :] = part.astype(BF16)


def backward(count, mixed, slope, rows, patch, window, wp_t):
    bands, _, depth, slots = mixed.shape
    head_ch, channels = wp_t.shape
    taps = patch.shape[1]
    out_rows = taps + 6 * head_ch
    each = lambda i, *_: (i, 0)
    total = bands * slots
    group = GROUP if bands % GROUP == 0 else 1
    return pl.pallas_call(
        backward_kernel,
        out_shape=jax.ShapeDtypeStruct((out_rows, channels), BF16),
        grid_spec=pltpu.PrefetchScalarGridSpec(
            num_scalar_prefetch=1,
            grid=(bands // group,),
            in_specs=[
                pl.BlockSpec((group, 1, depth, slots), lambda i, *_: (i, 1, 0, 0)),
                pl.BlockSpec((group, 1, depth, slots), lambda i, *_: (i, 0, 0, 0)),
                pl.BlockSpec((group * slots, channels), each),
                pl.BlockSpec((group * slots, channels), each),
                pl.BlockSpec((group * slots, taps), each),
                pl.BlockSpec((group * slots, window.shape[1]), each),
                pl.BlockSpec(wp_t.shape, lambda i, *_: (0, 0)),
            ],
            out_specs=pl.BlockSpec((out_rows, channels), lambda i, *_: (0, 0)),
            scratch_shapes=[
                pltpu.VMEM((channels, taps), F32),
                pltpu.VMEM((head_ch, channels), F32),
                pltpu.VMEM((head_ch, window.shape[1]), F32),
            ],
        ),
        compiler_params=pltpu.CompilerParams(
            dimension_semantics=("arbitrary",), vmem_limit_bytes=20 << 20
        ),
        cost_estimate=pl.CostEstimate(
            flops=2 * total * taps * channels, bytes_accessed=10 << 20, transcendentals=0
        ),
        name="backward",
    )(count, mixed, mixed, slope, rows, patch, window, wp_t)


def unpack_kernel(sectors, *refs):
    *held, range_ref, proj_ref, head_ref, sums = refs
    cores = len(held)
    pieces, height, _ = held[0].shape
    taps = range_ref.shape[0]
    head_ch = proj_ref.shape[0]
    me = lax.axis_index("core")
    for core in range(cores):

        @pl.when(me == core)
        def _():
            for k in range(cores):
                whose = (core - k) % cores
                for piece in range(pieces):
                    pair, sector = divmod(piece, sectors)
                    start = ((pair * cores + whose) * sectors + sector) * height
                    sums[pl.ds(start, height), :] = held[k][piece].astype(F32)

    range_ref[...] = sums[pl.ds(0, taps), :]
    proj_ref[...] = sums[pl.ds(taps, head_ch), :]
    for a in range(3):
        for b in range(3):
            block, half = (b, a) if a < 2 else ((3, b) if b < 2 else (4, 1))
            start = taps + head_ch * (block + 1)
            part = sums[pl.ds(start, head_ch), :]
            head_ref[2 - a, 2 - b] = part[:, half * head_ch : (half + 1) * head_ch]


def unpack(held, taps, head_ch):
    vmem = pl.BlockSpec(memory_space=pltpu.VMEM)
    pieces, height, channels = held[0].shape
    return pl.pallas_call(
        functools.partial(unpack_kernel, lax.axis_size("sector")),
        out_shape=(
            jax.ShapeDtypeStruct((taps, channels), F32),
            jax.ShapeDtypeStruct((head_ch, channels), F32),
            jax.ShapeDtypeStruct((3, 3, head_ch, head_ch), F32),
        ),
        in_specs=[vmem] * len(held),
        out_specs=(vmem, vmem, vmem),
        scratch_shapes=[pltpu.VMEM((len(held) * pieces * height, channels), F32)],
        compiler_params=pltpu.CompilerParams(vmem_limit_bytes=6 << 20),
        name="unpack",
    )(*held)


def place_kernel(tile_ref, rows_ref, out_ref, acc):
    tiles, head_ch, cells = acc.shape
    lists, _, slots = rows_ref.shape
    per_list = tile_ref.shape[0] // lists
    slot_len = slots // per_list
    acc[...] = jnp.zeros_like(acc)

    def body(step, _):
        for k in range(per_list):
            tile = tile_ref[step * per_list + k]

            @pl.when(jnp.logical_and(tile >= 0, tile < tiles))
            def _():
                part = rows_ref[step, :, k * slot_len : (k + 1) * slot_len]
                target = part[head_ch : head_ch + 1].astype(F32).astype(jnp.int32)
                places = lax.broadcasted_iota(jnp.int32, (cells, slot_len), 0)
                hot = jnp.where(places == target, 1.0, 0.0).astype(BF16)
                acc[tile] += dot(part[:head_ch], hot, NT)

        return 0

    lax.fori_loop(0, lists, body, 0)
    out_ref[...] = acc[...].astype(BF16)


def place(tiles, rows, count, head_ch):
    lists, _, slots = rows.shape
    return pl.pallas_call(
        place_kernel,
        out_shape=jax.ShapeDtypeStruct((count, head_ch, CELLS), BF16),
        in_specs=[
            pl.BlockSpec(memory_space=pltpu.SMEM),
            pl.BlockSpec(memory_space=pltpu.VMEM),
        ],
        out_specs=pl.BlockSpec(memory_space=pltpu.VMEM),
        scratch_shapes=[pltpu.VMEM((count, head_ch, CELLS), F32)],
        compiler_params=pltpu.CompilerParams(vmem_limit_bytes=12 << 20),
        cost_estimate=pl.CostEstimate(
            flops=2 * lists * slots * head_ch * CELLS, bytes_accessed=2 << 20, transcendentals=0
        ),
        name="place",
    )(tiles, rows)


def gathered(block, axis):
    count = lax.axis_size(axis)
    places = jnp.arange(count, dtype=jnp.int32)
    if count & (count - 1):
        return lax.all_gather(block, axis), places
    held = block[None]
    bit = count // 2
    while bit:
        other = lax.ppermute(held, axis, [(i, i ^ bit) for i in range(count)])
        held = jnp.stack([held, other], axis=1).reshape((-1,) + block.shape)
        bit //= 2
    return held, places ^ lax.axis_index(axis)


def exchanged(block, axis):
    count = lax.axis_size(axis)
    places = jnp.arange(count, dtype=jnp.int32)
    steps = []
    for k in range(1, count):
        ring = [(i, (i + k) % count) for i in range(count)]
        steps.append(lax.ppermute(block, axis, ring))
    return jnp.stack([block] + steps), (lax.axis_index(axis) - places) % count


def summed(rows):
    axes = SWEEP + ("sector",)
    count = lax.axis_size(axes)
    pieces = rows.reshape(count, rows.shape[0] // count, rows.shape[1])
    parts = lax.all_to_all(pieces, axes, split_axis=0, concat_axis=0, tiled=True)
    total = parts.astype(F32).sum(axis=0).astype(BF16)
    cores = lax.axis_size("core")
    spread = jnp.broadcast_to(total[None], (count // cores,) + total.shape)
    spread = lax.all_to_all(
        spread, ("pair", "sector"), split_axis=0, concat_axis=0, tiled=True
    )
    held = [spread]
    for k in range(1, cores):
        ring = [(i, (i + k) % cores) for i in range(cores)]
        held.append(lax.ppermute(spread, "core", ring))
    return held


def shards(
    range_image, send_pixel, send_cell, send_tile, send_count, w_range, w_proj, w_head, cotangent
):
    image = pltpu.with_memory_space_constraint(range_image[0], pltpu.HBM)
    beams, columns, channels = image.shape
    head_ch, grid_rows, grid_cols = cotangent.shape
    count = send_count[0, 0]
    pixels, cells, tiles = send_pixel[0, 0], send_cell[0, 0], send_tile[0, 0]
    _, slots = pixels.shape
    per_list = tiles.shape[1]
    sectors = lax.axis_size("sector")
    sweeps = lax.axis_size(SWEEP)
    sweep = lax.axis_index(SWEEP)
    slot_tiles = jnp.repeat(tiles, slots // per_list, axis=1)

    ahead, behind, cot_lines = edges(image, pltpu.with_memory_space_constraint(cotangent, pltpu.HBM))
    ring = [(i, (i + 1) % sectors) for i in range(sectors)]
    from_left = lax.ppermute(ahead, "sector", ring)
    from_right = lax.ppermute(behind, "sector", [(j, i) for i, j in ring])
    targets = slot_tiles * CELLS + cells
    targets_in = lax.all_to_all(targets, "sector", split_axis=0, concat_axis=0, tiled=True)

    base = (pixels // columns) * (columns + 2 * EDGE) + pixels % columns + EDGE - 1
    wp_t = w_proj.T
    lines = jnp.concatenate(
        [from_left[beams:][None], cot_lines, from_right[beams:][None]], axis=0
    )
    band_cot, order = exchanged(lines, SWEEP)
    patch, slope, rows, send = forward(
        base, count, image, from_left, from_right, w_range.reshape(-1, channels), wp_t
    )

    targets_in, send = lax.optimization_barrier((targets_in, send))
    band_pitch = sweeps * grid_cols + 2 * EDGE
    cell_in = targets_in % CELLS
    column_in = (targets_in // CELLS) * TILE + cell_in % TILE
    pick_base = (cell_in // TILE) * band_pitch + column_in + EDGE - 1
    flipped = w_head[::-1, ::-1].transpose(2, 0, 1, 3)
    pair_low = jnp.concatenate([flipped[:, 0], flipped[:, 1]], axis=-1)
    pair_high = jnp.concatenate([jnp.zeros_like(flipped[:, 2]), flipped[:, 2]], axis=-1)
    wg = jnp.stack([pair_low, pair_high], axis=1).reshape(head_ch, -1)
    window, send = pick(pick_base, order, band_cot, wg, send)
    targets_in, send = lax.optimization_barrier((targets_in, send))
    index_rows = jnp.stack([targets_in % CELLS, targets_in // CELLS], axis=1).astype(BF16)
    index_rows = jnp.pad(index_rows, ((0, 0), (0, IDX_ROWS - 2), (0, 0)))
    index_rows, send, window = lax.optimization_barrier((index_rows, send, window))
    mixed = lax.all_to_all(send, "sector", split_axis=0, concat_axis=0, tiled=True)
    sent_in = jnp.concatenate([mixed[:, 0], index_rows], axis=1)

    lists, _ = gathered(sent_in, SWEEP)
    lists = lists.reshape((-1,) + sent_in.shape[1:])
    owned = grid_cols // TILE
    tile_rows = lists[:, head_ch + 1, :: slots // per_list].astype(jnp.int32).reshape(-1)
    ground = place(tile_rows - (sweep * owned - 1), lists, owned + 2, head_ch)
    local = backward(count, mixed, slope, rows, patch, window, wp_t)
    held = summed(local)
    taps = w_range.shape[0] * w_range.shape[1] * channels
    grad_range, grad_proj, grad_head = unpack(held, taps, head_ch)
    grad_range = grad_range.reshape(w_range.shape)
    grad_proj = grad_proj.T

    ground = (
        ground.reshape(owned + 2, head_ch, TILE, TILE)
        .transpose(1, 2, 0, 3)
        .reshape(head_ch, TILE, (owned + 2) * TILE)[:, :, TILE - 1 : TILE + grid_cols + 1]
    )
    over = lax.ppermute(ground[:, -1:], "sector", ring[:-1])
    under = lax.ppermute(ground[:, :1], "sector", [(j, i) for i, j in ring[:-1]])
    head_sum = jnp.zeros((head_ch, grid_rows * grid_cols), F32)
    for row_off in (1, 0, 2):
        block = ground
        if row_off == 0:
            block = jnp.concatenate([over, ground[:, :-1]], axis=1)
        elif row_off == 2:
            block = jnp.concatenate([ground[:, 1:], under], axis=1)
        for col_off in range(3):
            view = block[:, :, col_off : col_off + grid_cols].reshape(head_ch, -1)
            head_sum = head_sum + dot(w_head[row_off, col_off].T, view)
    head_out = head_sum.astype(BF16).reshape(head_ch, grid_rows, grid_cols)
    return head_out, grad_range, grad_proj, grad_head


def solution(mesh):
    sweeps, sectors = mesh.devices.shape
    cores = 2 if sweeps % 2 == 0 else 1
    devices = mesh.devices.reshape(sweeps // cores, cores, sectors)
    split = jax.sharding.Mesh(devices, SWEEP + ("sector",))
    return jax.shard_map(
        shards,
        mesh=split,
        in_specs=(
            P(SWEEP, None, "sector", None),
            P(SWEEP, "sector", None, None),
            P(SWEEP, "sector", None, None),
            P(SWEEP, "sector", None, None),
            P(SWEEP, "sector", None),
            P(),
            P(),
            P(),
            P(None, "sector", SWEEP),
        ),
        out_specs=(P(None, "sector", SWEEP), P(), P(), P()),
        check_vma=False,
    )
```

```python
import functools

import jax
import jax.numpy as jnp
from jax import lax
from jax.experimental import pallas as pl
from jax.experimental.pallas import tpu as pltpu
from jax.sharding import PartitionSpec as P


TILE = 16
CELLS = TILE * TILE
EDGE = 8
WIDE = 4
IDX_ROWS = 8
SWEEP = ("pair", "core")
GROUP = 8
BF16 = jnp.bfloat16
F32 = jnp.float32
NT = (((1,), (1,)), ((), ()))
TN = (((0,), (0,)), ((), ()))


def dot(a, b, dims=(((1,), (0,)), ((), ()))):
    return lax.dot_general(a, b, dims, preferred_element_type=F32)


def gather_slot(base_ref, table, picked, first, slot, slots, lines, pitch):
    base = base_ref[first + slot]
    for line in range(lines):
        at = (line * slots + slot) * WIDE
        if not isinstance(at, int):
            at = pl.multiple_of(at, WIDE)
        picked[pl.ds(at, WIDE), :] = table[pl.ds(base + line * pitch, WIDE), :]


def gather_windows(base_ref, table, picked, first, slots, lines, pitch):
    def body(step, _):
        for k in range(8):
            gather_slot(base_ref, table, picked, first, step * 8 + k, slots, lines, pitch)
        return 0

    lax.fori_loop(0, slots // 8, body, 0)


def in_turn(step, lists, slots, base_ref, table, buffers, lines, pitch, compute):
    now = step - 1
    first = jnp.minimum(step, lists - 1) * slots
    for parity in range(2):

        @pl.when(jnp.logical_and(step > 0, lax.rem(now, 2) == parity))
        def _():
            for slot in range(slots):
                gather_slot(
                    base_ref, table, buffers[1 - parity], first, slot, slots, lines, pitch
                )
            compute(now, buffers[parity])


def plane(picked, slots, line, tap):
    return picked[pl.ds(line * slots * WIDE + tap, slots, stride=WIDE), :]


def edges_kernel(sectors, image_ref, cot_ref, ahead_ref, behind_ref, lines_ref, raw, cot, wide, sem):
    beams, columns, channels = image_ref.shape
    head_ch, rows, grid_cols = cot_ref.shape
    span = raw.shape[2]
    sector = lax.axis_index("sector")
    cot_copy = pltpu.make_async_copy(cot_ref, cot, sem.at[2])
    cot_copy.start()
    copies = []
    for k, first in enumerate((0, columns - span)):
        part = image_ref.at[:, pl.ds(first, span), :]
        copy = pltpu.make_async_copy(part, raw.at[k], sem.at[k])
        copy.start()
        copies.append(copy)
    cot_copy.wait()
    wide[pl.ds(0, head_ch * rows), :] = cot[...].astype(F32).reshape(head_ch * rows, grid_cols)
    for row in range(rows):
        line = wide[pl.ds(row, head_ch, stride=rows), :].astype(BF16)
        lines_ref[row] = line
        if row == 0:
            behind_ref[pl.ds(beams, head_ch), :] = jnp.where(sector > 0, line, 0)
        if row == rows - 1:
            ahead_ref[pl.ds(beams, head_ch), :] = jnp.where(sector < sectors - 1, line, 0)
    for k, (out_ref, at) in enumerate(((behind_ref, 0), (ahead_ref, span - 1))):
        copies[k].wait()
        wide[pl.ds(0, beams * span), :] = raw[k].astype(F32).reshape(beams * span, channels)
        out_ref[pl.ds(0, beams), :] = wide[pl.ds(at, beams, stride=span), :].astype(BF16)


def edges(image, cot):
    beams, _, channels = image.shape
    head_ch, rows, grid_cols = cot.shape
    edge = jax.ShapeDtypeStruct((beams + head_ch, channels), BF16)
    vmem = pl.BlockSpec(memory_space=pltpu.VMEM)
    return pl.pallas_call(
        functools.partial(edges_kernel, lax.axis_size("sector")),
        out_shape=(edge, edge, jax.ShapeDtypeStruct((rows, head_ch, grid_cols), BF16)),
        in_specs=[pl.BlockSpec(memory_space=pltpu.HBM)] * 2,
        out_specs=(vmem, vmem, vmem),
        scratch_shapes=[
            pltpu.VMEM((2, beams, TILE, channels), BF16),
            pltpu.VMEM(cot.shape, BF16),
            pltpu.VMEM((max(beams * TILE, head_ch * rows) + EDGE, channels), F32),
            pltpu.SemaphoreType.DMA((3,)),
        ],
        compiler_params=pltpu.CompilerParams(vmem_limit_bytes=4 << 20),
        name="edges",
    )(image, cot)


def forward_kernel(
    base_ref, count_ref, image_ref, left_ref, right_ref, w_ref, wp_ref,
    patch_ref, slope_ref, rows_ref, send_ref, raw, table, ends, even, odd, sem,
):
    step = pl.program_id(0)
    beams, columns, channels = image_ref.shape
    pitch = columns + 2 * EDGE
    slots = rows_ref.shape[0]
    chunks = raw.shape[0] // 8

    @pl.when(step == 0)
    def _():
        copies = []
        for c in range(chunks):
            part = pl.ds(c * 8, 8)
            copy = pltpu.make_async_copy(image_ref.at[part], raw.at[part], sem.at[c])
            copy.start()
            copies.append(copy)
        blank = jnp.zeros((pitch, channels), F32)
        table[pl.ds(0, pitch), :] = blank
        table[pl.ds((beams + 1) * pitch, pitch), :] = blank
        ends[0, pl.ds(0, beams), :] = left_ref[pl.ds(0, beams), :].astype(F32)
        ends[1, pl.ds(0, beams), :] = right_ref[pl.ds(0, beams), :].astype(F32)

        def sides(beam, _):
            line = (beam + 1) * pitch
            table[pl.ds(line + EDGE - 1, 1), :] = ends[0, pl.ds(beam, 1), :]
            table[pl.ds(line + EDGE + columns, 1), :] = ends[1, pl.ds(beam, 1), :]
            return 0

        lax.fori_loop(0, beams, sides, 0, unroll=8)
        for c in range(chunks):
            copies[c].wait()

            def widen(k, _):
                beam = c * 8 + k
                start = pl.multiple_of((beam + 1) * pitch + EDGE, 8)
                table[pl.ds(start, columns), :] = raw[beam].astype(F32)
                return 0

            lax.fori_loop(0, 8, widen, 0)
        gather_windows(base_ref, table, even, 0, slots, 3, pitch)

    def compute(band, picked):
        preact = None
        for k in range(0, 9, 2):
            parts = [plane(picked, slots, j // 3, j % 3) for j in range(k, min(k + 2, 9))]
            part = jnp.concatenate([p.astype(BF16) for p in parts], axis=1)
            columns = slice(k * channels, k * channels + part.shape[1])
            patch_ref[:, columns] = part
            term = dot(part, w_ref[columns, :])
            preact = term if preact is None else preact + term
        sigmoid = jax.nn.sigmoid(preact)
        slope_ref[...] = sigmoid * (1.0 + preact * (1.0 - sigmoid))
        live = lax.broadcasted_iota(jnp.int32, preact.shape, 0) < count_ref[band]
        rows = jnp.where(live, plane(picked, slots, 1, 1) + preact * sigmoid, 0.0).astype(BF16)
        rows_ref[...] = rows
        send_ref[0, 0] = dot(wp_ref[...], rows, NT).astype(BF16)

    lists = pl.num_programs(0) - 1
    in_turn(step, lists, slots, base_ref, table, (even, odd), 3, pitch, compute)


def forward(base, count, image, left, right, w_flat, wp_t):
    beams, columns, channels = image.shape
    bands, slots = base.shape
    head_ch = wp_t.shape[0]
    pitch = columns + 2 * EDGE
    taps = w_flat.shape[0]
    late = lambda i, *_: (jnp.maximum(i - 1, 0), 0)
    late4 = lambda i, *_: (jnp.maximum(i - 1, 0), 0, 0, 0)
    whole = lambda i, *_: (0, 0)
    total = bands * slots
    return pl.pallas_call(
        forward_kernel,
        out_shape=(
            jax.ShapeDtypeStruct((total, taps), BF16),
            jax.ShapeDtypeStruct((total, channels), F32),
            jax.ShapeDtypeStruct((total, channels), BF16),
            jax.ShapeDtypeStruct((bands, 2, head_ch, slots), BF16),
        ),
        grid_spec=pltpu.PrefetchScalarGridSpec(
            num_scalar_prefetch=2,
            grid=(bands + 1,),
            in_specs=[
                pl.BlockSpec(memory_space=pltpu.HBM),
                pl.BlockSpec(left.shape, whole),
                pl.BlockSpec(right.shape, whole),
                pl.BlockSpec(w_flat.shape, whole),
                pl.BlockSpec(wp_t.shape, whole),
            ],
            out_specs=[
                pl.BlockSpec((slots, taps), late),
                pl.BlockSpec((slots, channels), late),
                pl.BlockSpec((slots, channels), late),
                pl.BlockSpec((1, 1, head_ch, slots), late4),
            ],
            scratch_shapes=[
                pltpu.VMEM((beams, columns, channels), BF16),
                pltpu.VMEM(((beams + 2) * pitch + EDGE, channels), F32),
                pltpu.VMEM((2, beams + EDGE, channels), F32),
                pltpu.VMEM((3 * slots * WIDE + EDGE, channels), F32),
                pltpu.VMEM((3 * slots * WIDE + EDGE, channels), F32),
                pltpu.SemaphoreType.DMA((beams // 8,)),
            ],
        ),
        compiler_params=pltpu.CompilerParams(
            dimension_semantics=("arbitrary",), vmem_limit_bytes=24 << 20
        ),
        cost_estimate=pl.CostEstimate(
            flops=2 * total * taps * channels, bytes_accessed=24 << 20, transcendentals=0
        ),
        name="forward",
    )(base.reshape(-1), count, image, left, right, w_flat, wp_t)


def pick_kernel(
    base_ref, order_ref, cot_ref, wg_ref, send_ref, window_ref, grad_ref, table, even, odd
):
    step = pl.program_id(0)
    groups, lines, head_ch, columns = cot_ref.shape
    pitch = groups * columns + 2 * EDGE
    slots = window_ref.shape[0]

    @pl.when(step == 0)
    def _():
        blank = jnp.zeros((EDGE, 2 * head_ch), F32)

        def build(line, _):
            start = pl.multiple_of(line * pitch, 8)
            table[pl.ds(start, EDGE), :] = blank
            table[pl.ds(start + EDGE + groups * columns, EDGE), :] = blank
            for group in range(groups):
                held = order_ref[group]
                pair = jnp.concatenate([cot_ref[held, line], cot_ref[held, line + 1]], axis=0)
                at = pl.multiple_of(start + EDGE + group * columns, 8)
                table[pl.ds(at, columns), :] = pair.astype(F32).T
            return 0

        lax.fori_loop(0, lines - 1, build, 0)
        gather_windows(base_ref, table, even, 0, slots, 2, pitch)

    def compute(_, picked):
        parts = [plane(picked, slots, line, tap) for line in range(2) for tap in range(3)]
        window = jnp.concatenate([p.astype(BF16) for p in parts], axis=1)
        window_ref[...] = window
        grad_ref[0, 0] = dot(wg_ref[...], window, NT).astype(BF16)

    lists = pl.num_programs(0) - 1
    in_turn(step, lists, slots, base_ref, table, (even, odd), 2, pitch, compute)


def pick(base, order, band_cot, wg, send):
    groups, lines, head_ch, columns = band_cot.shape
    sectors, slots = base.shape
    pitch = groups * columns + 2 * EDGE
    late = lambda i, *_: (jnp.maximum(i - 1, 0), 0)
    late4 = lambda i, *_: (jnp.maximum(i - 1, 0), 1, 0, 0)
    total = sectors * slots
    return pl.pallas_call(
        pick_kernel,
        out_shape=(
            jax.ShapeDtypeStruct((total, 12 * head_ch), BF16),
            jax.ShapeDtypeStruct(send.shape, BF16),
        ),
        grid_spec=pltpu.PrefetchScalarGridSpec(
            num_scalar_prefetch=2,
            grid=(sectors + 1,),
            in_specs=[
                pl.BlockSpec(band_cot.shape, lambda i, *_: (0, 0, 0, 0)),
                pl.BlockSpec(wg.shape, lambda i, *_: (0, 0)),
                pl.BlockSpec(memory_space=pl.ANY),
            ],
            out_specs=[
                pl.BlockSpec((slots, 12 * head_ch), late),
                pl.BlockSpec((1, 1) + send.shape[2:], late4),
            ],
            scratch_shapes=[
                pltpu.VMEM(((lines - 1) * pitch + EDGE, 2 * head_ch), F32),
                pltpu.VMEM((2 * slots * WIDE + EDGE, 2 * head_ch), F32),
                pltpu.VMEM((2 * slots * WIDE + EDGE, 2 * head_ch), F32),
            ],
        ),
        input_output_aliases={4: 1},
        compiler_params=pltpu.CompilerParams(
            dimension_semantics=("arbitrary",), vmem_limit_bytes=14 << 20
        ),
        cost_estimate=pl.CostEstimate(
            flops=24 * total * head_ch * head_ch, bytes_accessed=12 << 20, transcendentals=0
        ),
        name="pick",
    )(base.reshape(-1), order, band_cot, wg, send)


def backward_kernel(
    count_ref, back_ref, sent_ref, slope_ref, rows_ref, patch_ref, window_ref, wp_ref,
    out_ref, range_acc, proj_acc, head_acc,
):
    step = pl.program_id(0)
    head_ch = wp_ref.shape[0]
    channels = rows_ref.shape[1]
    group = back_ref.shape[0]

    @pl.when(step == 0)
    def _():
        range_acc[...] = jnp.zeros_like(range_acc)
        proj_acc[...] = jnp.zeros_like(proj_acc)
        head_acc[...] = jnp.zeros_like(head_acc)

    lists = []
    for k in range(group):
        grads = back_ref[k, 0]
        live = lax.broadcasted_iota(jnp.int32, grads.shape, 1) < count_ref[step * group + k]
        lists.append(jnp.where(live, grads.astype(F32), 0.0).astype(BF16))
    grads = jnp.concatenate(lists, axis=1)
    sent = jnp.concatenate([sent_ref[k, 0] for k in range(group)], axis=1)
    hidden_grad = dot(grads, wp_ref[...], TN)
    preact_grad = (hidden_grad * slope_ref[...]).T.astype(BF16)
    range_acc[...] += dot(preact_grad, patch_ref[...])
    proj_acc[...] += dot(grads, rows_ref[...])
    head_acc[...] += dot(sent, window_ref[...])

    @pl.when(step == pl.num_programs(0) - 1)
    def _():
        taps = range_acc.shape[1] // channels
        for k in range(taps):
            out_ref[pl.ds(k * channels, channels), :] = (
                range_acc[:, k * channels : (k + 1) * channels].T.astype(BF16)
            )
        at = taps * channels
        out_ref[pl.ds(at, head_ch), :] = proj_acc[...].astype(BF16)
        wide = 2 * head_ch
        block = [head_acc[:, k * wide : (k + 1) * wide] for k in range(6)]
        first = lax.broadcasted_iota(jnp.int32, (head_ch, wide), 1) < head_ch
        both = jnp.where(first, pltpu.roll(block[3], head_ch, 1), block[4])
        for k, part in enumerate((block[0], block[1], block[2], both, block[5])):
            start = at + head_ch * (k + 1)
            out_ref[pl.ds(start, head_ch), :] = part.astype(BF16)


def backward(count, mixed, slope, rows, patch, window, wp_t):
    bands, _, depth, slots = mixed.shape
    head_ch, channels = wp_t.shape
    taps = patch.shape[1]
    out_rows = taps + 6 * head_ch
    each = lambda i, *_: (i, 0)
    total = bands * slots
    group = GROUP if bands % GROUP == 0 else 1
    return pl.pallas_call(
        backward_kernel,
        out_shape=jax.ShapeDtypeStruct((out_rows, channels), BF16),
        grid_spec=pltpu.PrefetchScalarGridSpec(
            num_scalar_prefetch=1,
            grid=(bands // group,),
            in_specs=[
                pl.BlockSpec((group, 1, depth, slots), lambda i, *_: (i, 1, 0, 0)),
                pl.BlockSpec((group, 1, depth, slots), lambda i, *_: (i, 0, 0, 0)),
                pl.BlockSpec((group * slots, channels), each),
                pl.BlockSpec((group * slots, channels), each),
                pl.BlockSpec((group * slots, taps), each),
                pl.BlockSpec((group * slots, window.shape[1]), each),
                pl.BlockSpec(wp_t.shape, lambda i, *_: (0, 0)),
            ],
            out_specs=pl.BlockSpec((out_rows, channels), lambda i, *_: (0, 0)),
            scratch_shapes=[
                pltpu.VMEM((channels, taps), F32),
                pltpu.VMEM((head_ch, channels), F32),
                pltpu.VMEM((head_ch, window.shape[1]), F32),
            ],
        ),
        compiler_params=pltpu.CompilerParams(
            dimension_semantics=("arbitrary",), vmem_limit_bytes=28 << 20
        ),
        cost_estimate=pl.CostEstimate(
            flops=2 * total * taps * channels, bytes_accessed=10 << 20, transcendentals=0
        ),
        name="backward",
    )(count, mixed, mixed, slope, rows, patch, window, wp_t)


def unpack_kernel(sectors, *refs):
    *held, range_ref, proj_ref, head_ref, sums = refs
    cores = len(held)
    pieces, height, _ = held[0].shape
    taps = range_ref.shape[0]
    head_ch = proj_ref.shape[0]
    me = lax.axis_index("core")
    for core in range(cores):

        @pl.when(me == core)
        def _():
            for k in range(cores):
                whose = (core - k) % cores
                for piece in range(pieces):
                    pair, sector = divmod(piece, sectors)
                    start = ((pair * cores + whose) * sectors + sector) * height
                    sums[pl.ds(start, height), :] = held[k][piece].astype(F32)

    range_ref[...] = sums[pl.ds(0, taps), :]
    proj_ref[...] = sums[pl.ds(taps, head_ch), :]
    for a in range(3):
        for b in range(3):
            block, half = (b, a) if a < 2 else ((3, b) if b < 2 else (4, 1))
            start = taps + head_ch * (block + 1)
            part = sums[pl.ds(start, head_ch), :]
            head_ref[2 - a, 2 - b] = part[:, half * head_ch : (half + 1) * head_ch]


def unpack(held, taps, head_ch):
    vmem = pl.BlockSpec(memory_space=pltpu.VMEM)
    pieces, height, channels = held[0].shape
    return pl.pallas_call(
        functools.partial(unpack_kernel, lax.axis_size("sector")),
        out_shape=(
            jax.ShapeDtypeStruct((taps, channels), F32),
            jax.ShapeDtypeStruct((head_ch, channels), F32),
            jax.ShapeDtypeStruct((3, 3, head_ch, head_ch), F32),
        ),
        in_specs=[vmem] * len(held),
        out_specs=(vmem, vmem, vmem),
        scratch_shapes=[pltpu.VMEM((len(held) * pieces * height, channels), F32)],
        compiler_params=pltpu.CompilerParams(vmem_limit_bytes=6 << 20),
        name="unpack",
    )(*held)


def place_kernel(tile_ref, rows_ref, out_ref, acc):
    tiles, head_ch, cells = acc.shape
    lists, _, slots = rows_ref.shape
    per_list = tile_ref.shape[0] // lists
    slot_len = slots // per_list
    acc[...] = jnp.zeros_like(acc)

    def body(step, _):
        for k in range(per_list):
            tile = tile_ref[step * per_list + k]

            @pl.when(jnp.logical_and(tile >= 0, tile < tiles))
            def _():
                part = rows_ref[step, :, k * slot_len : (k + 1) * slot_len]
                target = part[head_ch : head_ch + 1].astype(F32).astype(jnp.int32)
                places = lax.broadcasted_iota(jnp.int32, (cells, slot_len), 0)
                hot = jnp.where(places == target, 1.0, 0.0).astype(BF16)
                acc[tile] += dot(part[:head_ch], hot, NT)

        return 0

    lax.fori_loop(0, lists, body, 0)
    out_ref[...] = acc[...].astype(BF16)


def place(tiles, rows, count, head_ch):
    lists, _, slots = rows.shape
    return pl.pallas_call(
        place_kernel,
        out_shape=jax.ShapeDtypeStruct((count, head_ch, CELLS), BF16),
        in_specs=[
            pl.BlockSpec(memory_space=pltpu.SMEM),
            pl.BlockSpec(memory_space=pltpu.VMEM),
        ],
        out_specs=pl.BlockSpec(memory_space=pltpu.VMEM),
        scratch_shapes=[pltpu.VMEM((count, head_ch, CELLS), F32)],
        compiler_params=pltpu.CompilerParams(vmem_limit_bytes=12 << 20),
        cost_estimate=pl.CostEstimate(
            flops=2 * lists * slots * head_ch * CELLS, bytes_accessed=2 << 20, transcendentals=0
        ),
        name="place",
    )(tiles, rows)


def gathered(block, axis):
    count = lax.axis_size(axis)
    places = jnp.arange(count, dtype=jnp.int32)
    if count & (count - 1):
        return lax.all_gather(block, axis), places
    held = block[None]
    bit = count // 2
    while bit:
        other = lax.ppermute(held, axis, [(i, i ^ bit) for i in range(count)])
        held = jnp.stack([held, other], axis=1).reshape((-1,) + block.shape)
        bit //= 2
    return held, places ^ lax.axis_index(axis)


def exchanged(block, axis):
    count = lax.axis_size(axis)
    places = jnp.arange(count, dtype=jnp.int32)
    steps = []
    for k in range(1, count):
        ring = [(i, (i + k) % count) for i in range(count)]
        steps.append(lax.ppermute(block, axis, ring))
    return jnp.stack([block] + steps), (lax.axis_index(axis) - places) % count


def summed(rows):
    axes = SWEEP + ("sector",)
    count = lax.axis_size(axes)
    pieces = rows.reshape(count, rows.shape[0] // count, rows.shape[1])
    parts = lax.all_to_all(pieces, axes, split_axis=0, concat_axis=0, tiled=True)
    total = parts.astype(F32).sum(axis=0).astype(BF16)
    cores = lax.axis_size("core")
    spread = jnp.broadcast_to(total[None], (count // cores,) + total.shape)
    spread = lax.all_to_all(
        spread, ("pair", "sector"), split_axis=0, concat_axis=0, tiled=True
    )
    held = [spread]
    for k in range(1, cores):
        ring = [(i, (i + k) % cores) for i in range(cores)]
        held.append(lax.ppermute(spread, "core", ring))
    return held


def shards(
    range_image, send_pixel, send_cell, send_tile, send_count, w_range, w_proj, w_head, cotangent
):
    image = pltpu.with_memory_space_constraint(range_image[0], pltpu.HBM)
    beams, columns, channels = image.shape
    head_ch, grid_rows, grid_cols = cotangent.shape
    count = send_count[0, 0]
    pixels, cells, tiles = send_pixel[0, 0], send_cell[0, 0], send_tile[0, 0]
    _, slots = pixels.shape
    per_list = tiles.shape[1]
    sectors = lax.axis_size("sector")
    sweeps = lax.axis_size(SWEEP)
    sweep = lax.axis_index(SWEEP)
    slot_tiles = jnp.repeat(tiles, slots // per_list, axis=1)

    ahead, behind, cot_lines = edges(image, pltpu.with_memory_space_constraint(cotangent, pltpu.HBM))
    ring = [(i, (i + 1) % sectors) for i in range(sectors)]
    from_left = lax.ppermute(ahead, "sector", ring)
    from_right = lax.ppermute(behind, "sector", [(j, i) for i, j in ring])
    targets = slot_tiles * CELLS + cells
    targets_in = lax.all_to_all(targets, "sector", split_axis=0, concat_axis=0, tiled=True)

    base = (pixels // columns) * (columns + 2 * EDGE) + pixels % columns + EDGE - 1
    wp_t = w_proj.T
    lines = jnp.concatenate(
        [from_left[beams:][None], cot_lines, from_right[beams:][None]], axis=0
    )
    band_cot, order = exchanged(lines, SWEEP)
    patch, slope, rows, send = forward(
        base, count, image, from_left, from_right, w_range.reshape(-1, channels), wp_t
    )

    targets_in, send = lax.optimization_barrier((targets_in, send))
    band_pitch = sweeps * grid_cols + 2 * EDGE
    cell_in = targets_in % CELLS
    column_in = (targets_in // CELLS) * TILE + cell_in % TILE
    pick_base = (cell_in // TILE) * band_pitch + column_in + EDGE - 1
    flipped = w_head[::-1, ::-1].transpose(2, 0, 1, 3)
    pair_low = jnp.concatenate([flipped[:, 0], flipped[:, 1]], axis=-1)
    pair_high = jnp.concatenate([jnp.zeros_like(flipped[:, 2]), flipped[:, 2]], axis=-1)
    wg = jnp.stack([pair_low, pair_high], axis=1).reshape(head_ch, -1)
    window, send = pick(pick_base, order, band_cot, wg, send)
    targets_in, send = lax.optimization_barrier((targets_in, send))
    index_rows = jnp.stack([targets_in % CELLS, targets_in // CELLS], axis=1).astype(BF16)
    index_rows = jnp.pad(index_rows, ((0, 0), (0, IDX_ROWS - 2), (0, 0)))
    index_rows, send, window = lax.optimization_barrier((index_rows, send, window))
    mixed = lax.all_to_all(send, "sector", split_axis=0, concat_axis=0, tiled=True)
    sent_in = jnp.concatenate([mixed[:, 0], index_rows], axis=1)

    lists, _ = gathered(sent_in, SWEEP)
    lists = lists.reshape((-1,) + sent_in.shape[1:])
    owned = grid_cols // TILE
    tile_rows = lists[:, head_ch + 1, :: slots // per_list].astype(jnp.int32).reshape(-1)
    ground = place(tile_rows - (sweep * owned - 1), lists, owned + 2, head_ch)
    local = backward(count, mixed, slope, rows, patch, window, wp_t)
    held = summed(local)
    taps = w_range.shape[0] * w_range.shape[1] * channels
    grad_range, grad_proj, grad_head = unpack(held, taps, head_ch)
    grad_range = grad_range.reshape(w_range.shape)
    grad_proj = grad_proj.T

    ground = (
        ground.reshape(owned + 2, head_ch, TILE, TILE)
        .transpose(1, 2, 0, 3)
        .reshape(head_ch, TILE, (owned + 2) * TILE)[:, :, TILE - 1 : TILE + grid_cols + 1]
    )
    over = lax.ppermute(ground[:, -1:], "sector", ring[:-1])
    under = lax.ppermute(ground[:, :1], "sector", [(j, i) for i, j in ring[:-1]])
    ground_pad = jnp.concatenate([over, ground, under], axis=1)
    head_sum = jnp.zeros((head_ch, grid_rows * grid_cols), F32)
    for row_off in (1, 0, 2):
        block = ground
        if row_off != 1:
            block = ground_pad[:, row_off : row_off + grid_rows]
        for col_off in range(3):
            view = block[:, :, col_off : col_off + grid_cols].reshape(head_ch, -1)
            head_sum = head_sum + dot(w_head[row_off, col_off].T, view)
    head_out = head_sum.astype(BF16).reshape(head_ch, grid_rows, grid_cols)
    return head_out, grad_range, grad_proj, grad_head


def solution(mesh):
    sweeps, sectors = mesh.devices.shape
    cores = 2 if sweeps % 2 == 0 else 1
    devices = mesh.devices.reshape(sweeps // cores, cores, sectors)
    split = jax.sharding.Mesh(devices, SWEEP + ("sector",))
    return jax.shard_map(
        shards,
        mesh=split,
        in_specs=(
            P(SWEEP, None, "sector", None),
            P(SWEEP, "sector", None, None),
            P(SWEEP, "sector", None, None),
            P(SWEEP, "sector", None, None),
            P(SWEEP, "sector", None),
            P(),
            P(),
            P(),
            P(None, "sector", SWEEP),
        ),
        out_specs=(P(None, "sector", SWEEP), P(), P(), P()),
        check_vma=False,
    )
```
